256 devices in a mesh: rows: 64 (over x, z, core), cols: 4 (over y).
Axes of the slice: x: 4, y: 4, z: 8, core: 2. Of those that a mesh axis runs over, the one named last changes fastest.
Arguments:
- slot_tile: int32 [64, 3], replicated, may hold values from 0 to 128, as said below
- slot_ranks: int32 [64, 3, 4], P('rows', None, 'cols'), may hold values from 0 to 256, as said below
- diag_ranks: int32 [4], P('cols'), may hold values from 32 to 256
- panel_left_factors: bfloat16 [4, 192, 1024, 256], P('cols', 'rows'), may hold values from -12 to 12
- panel_v: bfloat16 [4, 192, 1024, 256], P('cols', 'rows'), may hold values from -0.1875 to 0.1875
- diag_u: bfloat16 [4, 1024, 256], P('cols'), may hold values from -0.38 to 0.38, as said below
- diag_v: bfloat16 [4, 1024, 256], P('cols'), may hold values from -1 to 1
- panel_points: int32 [192, 2, 1024], P('rows', None, 'cols'), may hold values from 0 to 1023, as said below
- diag_points: int32 [2, 1024], replicated, may hold values from 0 to 1023, as said below
- rhs_diag: float32 [1024, 512], P(None, 'cols'), may hold values from -0.3 to 0.3
- rhs_rest: float32 [128, 4, 4, 64, 512], P(None, 'cols', None, 'rows'), may hold values from -6 to 6
Outputs:
- panel_factor: bfloat16 [192, 1024, 1024], P('rows', 'cols')
- diag_solution: float32 [1024, 512], P(None, 'cols')
- rhs_out: float32 [128, 4, 4, 64, 512], P(None, 'cols', None, 'rows')
The draws below stay inside these ranges and needn't reach their ends.
Inputs may be any that keep to these rules, and one draw needn't show every extreme that they name: `slot_tile`: every tile 0 to 127 stands in exactly one slot; 128 marks an empty slot; the live slots of an owner come first; every owner has 1 to 3 live slots and some owner has 3. Owners are chosen by the tiles' summed ranks. `slot_ranks`: live slots have ranks 32 to 256, empty slots 0; both 32 and 256 occur. The columns of each diag_u[j] are orthogonal, with lengths 0.1 to 0.38. `panel_points`: row 0 holds x, row 1 holds y. A live slot holds the cells of a block of 32 x (32) grid cells in some order; blocks of different tiles and of the diagonal tile are distinct; an empty slot holds the points of some tile. `diag_points`: row 0 holds x, row 1 holds y: the cells of one block of 32 x (32) grid cells in some order.
All inputs are finite; a program needn't handle non-finite values.
Results may differ from the reference program's by a relative error of at most 0.0057.
Values may be sent and summed in bfloat16 or wider, within the bound.
A program may use at most 128 MiB of HBM per device.

```python
import jax
import jax.numpy as jnp
from jax import lax

B = 1024
RMAX = 256
OUT = 512
TMAX = 3
GX = 1024
GY = 512
J = 4
NT = 128
SLOTS = 192
K = 4
N_ROWS = 64
N_COLS = 4


def shuffled(cell_key):
    return jax.random.permutation(cell_key, B)


def layout(key):
    base = jax.random.fold_in(key, 11)
    rank_key, device_key, block_key, cell_key, diag_key = jax.random.split(base, 5)
    tile_count = 2 * N_ROWS
    tile_ranks = jax.random.randint(rank_key, (tile_count, J), RMAX // 8, RMAX + 1, dtype=jnp.int32)
    tile_ranks = tile_ranks.at[0, 0].set(RMAX).at[1, J - 1].set(RMAX // 8)
    weight_sum = jnp.sum(tile_ranks, axis=1)
    sort_key = weight_sum * tile_count + jnp.arange(tile_count, dtype=jnp.int32)
    heavy_first = jnp.argsort(-sort_key).astype(jnp.int32)
    device_order = jax.random.permutation(device_key, N_ROWS).astype(jnp.int32)
    position = jnp.arange(tile_count, dtype=jnp.int32)
    single = N_ROWS // 4
    double_end = single + N_ROWS
    in_double = position - single
    triple_membership = position - double_end
    group_device = jnp.where(position < single, position, jnp.where(position < double_end, single + in_double // 2, single + N_ROWS // 2 + triple_membership // 3))
    group_slot = jnp.where(position < single, 0, jnp.where(position < double_end, in_double % 2, triple_membership % 3))
    device = device_order[group_device]
    slot_tile = jnp.full((N_ROWS, TMAX), tile_count, jnp.int32).at[device, group_slot].set(heavy_first)
    slot_ranks = jnp.zeros((N_ROWS, TMAX, J), jnp.int32).at[device, group_slot].set(tile_ranks[heavy_first])
    diag_ranks = jax.random.randint(diag_key, (J,), RMAX // 8, RMAX + 1, dtype=jnp.int32)
    diag_ranks = diag_ranks.at[0].set(RMAX)
    block_wide = 32
    block_tall = B // 32
    blocks_x = GX // block_wide
    blocks_y = GY // block_tall
    row_key, perm_key = jax.random.split(block_key)
    diag_entry = blocks_x - 1 + blocks_x * jax.random.randint(row_key, (), 0, blocks_y, dtype=jnp.int32)
    shuffled_blocks = jax.random.permutation(perm_key, blocks_x * blocks_y).astype(jnp.int32)
    leading = shuffled_blocks[:tile_count]
    others = jnp.where(leading == diag_entry, shuffled_blocks[tile_count], leading)
    selected_entries = jnp.concatenate([diag_entry[None], others]).astype(jnp.int32)
    cell_keys = jax.random.split(cell_key, tile_count + 1)
    cells = jax.vmap(shuffled)(cell_keys).astype(jnp.int32)
    point_x = (selected_entries % blocks_x)[:, None] * block_wide + cells % block_wide
    point_y = (selected_entries // blocks_x)[:, None] * block_tall + cells // block_wide
    points = jnp.stack([point_x, point_y], axis=1).astype(jnp.int32)
    slot_points = points[1 + jnp.minimum(slot_tile.reshape(-1), tile_count - 1)]
    return (slot_tile, slot_ranks, diag_ranks, slot_points, points[0])


def draw_slot_tile(key, part):
    return layout(key)[0]


def draw_slot_ranks(key, part):
    return layout(key)[1]


def draw_diag_ranks(key, part):
    return layout(key)[2]


def draw_panel_points(key, part):
    return layout(key)[3]


def draw_diag_points(key, part):
    return layout(key)[4]


def orthonormal(key, columns):
    gauss = jax.random.normal(key, (J, B, columns), jnp.float32)
    basis, upper = jnp.linalg.qr(gauss)
    return basis


def draw_diag_u(key, part):
    basis = orthonormal(jax.random.fold_in(key, 21), RMAX)
    scale_key = jax.random.fold_in(key, 22)
    lengths = jnp.exp(jax.random.uniform(scale_key, (J, RMAX), jnp.float32, jnp.log(0.1), jnp.log(0.38)))
    return (basis * lengths[:, None, :]).astype(jnp.bfloat16)


def draw_diag_v(key, part):
    basis = orthonormal(jax.random.fold_in(key, 31), RMAX + 1)
    own_columns = basis[:, :, :RMAX]
    shared_column = basis[:, :, RMAX]
    scale_key = jax.random.fold_in(key, 32)
    weight_key = jax.random.fold_in(key, 33)
    mixing = 4.0 / RMAX
    weights = jax.random.normal(weight_key, (J, RMAX), jnp.float32)
    lengths = jax.random.uniform(scale_key, (J, RMAX), jnp.float32, 0.5, 1.0)
    vectors = jnp.sqrt(1.0 - mixing) * own_columns + jnp.sqrt(mixing) * weights[:, None, :] * shared_column[:, :, None]
    return (vectors * lengths[:, None, :]).astype(jnp.bfloat16)


def shard_levels(stream_key, extent, pieces, least, top_value):
    gain = 1.0
    for dim, blocks in pieces:
        heights = jax.random.uniform(jax.random.fold_in(jax.random.fold_in(stream_key, 6), dim), (blocks,), jnp.float32, least / len(pieces), top_value / len(pieces))
        gain = gain * jnp.repeat(jnp.exp(heights), extent[dim] // blocks).reshape((-1,) + (1,) * (len(extent) - 1 - dim))
    return gain


def normal_values(stream_key, shape, spread, bound, cuts=(), kind=jnp.bfloat16):
    entries = jax.random.normal(stream_key, shape, jnp.float32) * spread
    if len(cuts) > 0:
        entries = shard_levels(stream_key, shape, cuts, -0.22, 0.18) * entries
    return jnp.clip(entries, min=-bound, max=bound).astype(kind)


def setup_inputs(seed: int = 0) -> dict:
    seeds = jax.random.split(jax.random.key(seed), 12)
    return {
        "slot_tile": draw_slot_tile(jax.random.fold_in(seeds[11], 71), 0),
        "slot_ranks": draw_slot_ranks(jax.random.fold_in(seeds[11], 71), 0),
        "diag_ranks": draw_diag_ranks(jax.random.fold_in(seeds[11], 71), 0),
        "panel_left_factors": normal_values(seeds[3], (J, SLOTS, B, RMAX), 2.0, 12.0, ((0, 4), (1, 64))),
        "panel_v": normal_values(seeds[4], (J, SLOTS, B, RMAX), B ** -0.5, 0.1875, ((0, 4), (1, 64))),
        "diag_u": draw_diag_u(jax.random.fold_in(seeds[11], 71), 0),
        "diag_v": draw_diag_v(jax.random.fold_in(seeds[11], 71), 0),
        "panel_points": draw_panel_points(jax.random.fold_in(seeds[11], 71), 0),
        "diag_points": draw_diag_points(jax.random.fold_in(seeds[11], 71), 0),
        "rhs_diag": normal_values(seeds[9], (B, OUT), 0.05, 0.3, ((1, 4),), jnp.float32),
        "rhs_rest": normal_values(seeds[10], (NT, N_COLS, K, N_ROWS, OUT), 1.0, 6.0, ((1, 4), (3, 64)), jnp.float32),
    }


length_scale = 0.3
nugget = 1.0

def matern(first_x, first_y, second_x, second_y):
    spacing = 1.0 / GX
    delta_x = (first_x - second_x) * spacing
    delta_y = (first_y - second_y) * spacing
    scaled = jnp.sqrt(3.0) * jnp.sqrt(delta_x * delta_x + delta_y * delta_y) / length_scale
    return (1.0 + scaled) * jnp.exp(-scaled)

def reference(slot_tile, slot_ranks, diag_ranks, panel_left_factors, panel_v, diag_u, diag_v, panel_points, diag_points, rhs_diag, rhs_rest):
    rank_index = jnp.arange(RMAX, dtype=jnp.int32)
    diag_mask = (rank_index[None, :] < diag_ranks[:, None]).astype(jnp.bfloat16)
    diagonal_left_factor = diag_u * diag_mask[:, None, :]
    diagonal_right_factor = diag_v * diag_mask[:, None, :]
    diag_core = jnp.einsum('jbr,jbq->jrq', diagonal_right_factor.astype(jnp.float32), diagonal_right_factor.astype(jnp.float32)).astype(jnp.bfloat16)
    diag_low = jnp.einsum('jbr,jrq->jbq', diagonal_left_factor.astype(jnp.float32), diag_core.astype(jnp.float32)).astype(jnp.bfloat16)
    diag_term = jnp.einsum('jbr,jcr->bc', diag_low.astype(jnp.float32), diagonal_left_factor.astype(jnp.float32))
    centre = diag_points.astype(jnp.float32)
    identity = jnp.eye(B, dtype=jnp.float32)
    own_block = matern(centre[0][:, None], centre[1][:, None], centre[0], centre[1])
    diag_system = own_block + nugget * identity - diag_term
    factor = jnp.linalg.cholesky(diag_system)
    inverse = jax.scipy.linalg.solve_triangular(factor, identity, lower=True)
    diag_solution = jnp.dot(inverse, rhs_diag, precision=lax.Precision.HIGHEST)
    forward = diag_solution.astype(jnp.bfloat16)

    def one_slot(slot_index):
        slot_row = slot_index // TMAX
        slot_col = slot_index % TMAX
        ranks_here = slot_ranks[slot_row, slot_col]
        slot_mask = (rank_index[None, :] < ranks_here[:, None]).astype(jnp.bfloat16)
        slot_left_factor = panel_left_factors[:, slot_index] * slot_mask[:, None, :]
        slot_right_factor = panel_v[:, slot_index] * slot_mask[:, None, :]
        inner_product_core = jnp.einsum('jbr,jbq->jrq', slot_right_factor.astype(jnp.float32), diagonal_right_factor.astype(jnp.float32)).astype(jnp.bfloat16)
        low_rows = jnp.einsum('jbr,jrq->jbq', slot_left_factor.astype(jnp.float32), inner_product_core.astype(jnp.float32)).astype(jnp.bfloat16)
        update_term = jnp.einsum('jbr,jcr->bc', low_rows.astype(jnp.float32), diagonal_left_factor.astype(jnp.float32))
        coords = panel_points[slot_index].astype(jnp.float32)
        generated = matern(coords[0][:, None], coords[1][:, None], centre[0], centre[1])
        live_mask = (slot_tile[slot_row, slot_col] < NT).astype(jnp.float32)
        system_rows = live_mask * (generated - update_term)
        solved = jnp.dot(system_rows, inverse.T, precision=lax.Precision.HIGHEST).astype(jnp.bfloat16)
        slot_product = jnp.dot(solved.astype(jnp.float32), forward.astype(jnp.float32), preferred_element_type=jnp.float32).astype(jnp.bfloat16)
        return (solved, slot_product)
    panel_factor, products = lax.map(one_slot, jnp.arange(SLOTS, dtype=jnp.int32))
    flat_tiles = slot_tile.reshape(-1)
    owner_slot = jnp.zeros((NT + 1,), jnp.int32).at[flat_tiles].set(jnp.arange(SLOTS, dtype=jnp.int32))[:NT]
    tile_products = products[owner_slot].reshape(NT, N_COLS, K, N_ROWS, OUT)
    rhs_out = rhs_rest - tile_products.astype(jnp.float32)
    return (panel_factor, diag_solution, rhs_out)
```

```python
import functools

import jax
import jax.numpy as jnp
from jax import lax
from jax.experimental import pallas as pl
from jax.experimental.pallas import tpu as pltpu
from jax.sharding import PartitionSpec as P

GX = 1024

length_scale = 0.3
nugget = 1.0
F32 = jnp.float32
BF = jnp.bfloat16
HI = lax.Precision.HIGHEST


def split2(x):
    hi = x.astype(BF)
    lo = (x - hi.astype(F32)).astype(BF)
    return hi, lo


def mm(a, b, dims):
    return lax.dot_general(a, b, (dims, ((), ())), preferred_element_type=F32)


def mm3(a, b, dims):
    ah, al = split2(a)
    bh, bl = split2(b)
    return mm(ah, bh, dims) + (mm(ah, bl, dims) + mm(al, bh, dims))


def factor_block(rows, lin_ref):
    n = len(rows)
    rows = list(rows)
    lane = lax.broadcasted_iota(jnp.int32, (8, 128), 1)
    sub = lax.broadcasted_iota(jnp.int32, (8, 128), 0)
    bs = lambda x, k: jnp.broadcast_to(x[k:k + 1, :], (8, 128))
    for b in range(n):
        inblock = (lane >= 8 * b) & (lane < 8 * b + 8)
        t = rows[b]
        c = [jnp.broadcast_to(t[:, 8 * b + k:8 * b + k + 1], (8, 128)) for k in range(8)]
        tm = jnp.where(inblock, (lane - 8 * b == sub).astype(F32), t)
        y = tm
        scale = jnp.ones((8, 128), F32)
        avec = jnp.ones((8, 128), F32)
        bvec = jnp.zeros((8, 128), F32)
        for k in range(0, 8, 2):
            ck, cl = c[k], c[k + 1]
            pa, pb, pc = bs(ck, k), bs(ck, k + 1), bs(cl, k + 1)
            det = pa * pc - pb * pb
            r = 1.0 / det
            ek = pc * ck - pb * cl
            fk = pa * cl - pb * ck
            wk, wl = ek * r, fk * r
            at_k, at_l = sub == k, sub == k + 1
            scale = jnp.where(at_k, pa, jnp.where(at_l, pa * det, scale))
            avec = jnp.where(at_l, pa, avec)
            bvec = jnp.where(at_l, pb, bvec)
            if k < 6:
                below = sub > k + 1
                y = y - jnp.where(below, wk * bs(y, k) + wl * bs(y, k + 1), 0.0)
            new = list(c)
            for m in range(8):
                if m in (k, k + 1):
                    continue
                g = ck * bs(ek, m) + cl * bs(fk, m)
                v = c[m] - g * r
                new[m] = jnp.where(at_k, bs(wk, m), jnp.where(at_l, bs(wl, m), v))
            new[k] = jnp.where(at_k, -pc * r, jnp.where(at_l, pb * r, wk))
            new[k + 1] = jnp.where(at_k, pb * r, jnp.where(at_l, -pa * r, wl))
            c = new
        if b < n - 1:
            s = [c[m] * bs(tm, m) for m in range(8)]
            s = ((s[0] + s[1]) + (s[2] + s[3])) + ((s[4] + s[5]) + (s[6] + s[7]))
            sk = [bs(s, k) for k in range(8)]
            for i in range(b + 1, n):
                q = [jnp.broadcast_to(rows[i][:, 8 * b + k:8 * b + k + 1], (8, 128)) * sk[k] for k in range(8)]
                q = ((q[0] + q[1]) + (q[2] + q[3])) + ((q[4] + q[5]) + (q[6] + q[7]))
                rows[i] = jnp.where(inblock, 0.0, rows[i]) + q
        yy = avec * y - bvec * pltpu.roll(y, 1, 0)
        res = yy * lax.rsqrt(scale)
        lin_ref[8 * b:8 * b + 8, :] = jnp.where(lane < 8 * b + 8, res, 0.0)


def chol_inv_kernel(a_ref, x_ref, lin_ref, *, n, passes):
    nb = n // 128
    x_ref[...] = a_ref[...]
    dot = mm3 if passes == 3 else functools.partial(lambda a, b, dims: lax.dot_general(a, b, (dims, ((), ())), preferred_element_type=F32, precision=HI))

    def body(p, _):
        off = pl.multiple_of(p * 128, 128)
        rows = [x_ref[pl.ds(pl.multiple_of(off + 8 * b, 8), 8), pl.ds(off, 128)] for b in range(16)]
        factor_block(rows, lin_ref)
        lin = lin_ref[...]
        for q in range(nb):
            @pl.when(p == q)
            def _():
                lo, hi = 128 * q, 128 * (q + 1)
                left = None
                if q < nb - 1:
                    left = dot(x_ref[hi:, lo:hi], lin, ((1,), (1,)))
                    right = dot(lin, x_ref[lo:hi, hi:], ((1,), (0,)))
                    x_ref[lo:hi, hi:] = jnp.zeros((128, n - hi), F32)
                if q > 0:
                    x_ref[lo:hi, :lo] = dot(lin, x_ref[lo:hi, :lo], ((1,), (0,)))
                x_ref[lo:hi, lo:hi] = lin
                if q < nb - 1:
                    x_ref[hi:, hi:] = x_ref[hi:, hi:] - dot(left, right, ((1,), (0,)))
                    if q > 0:
                        x_ref[hi:, :lo] = x_ref[hi:, :lo] - dot(left, x_ref[lo:hi, :lo], ((1,), (0,)))
                    x_ref[hi:, lo:hi] = -dot(left, lin, ((1,), (0,)))
        return 0

    lax.fori_loop(0, nb, body, 0)


def chol_inv(a, passes=3):
    n = a.shape[0]
    return pl.pallas_call(
        functools.partial(chol_inv_kernel, n=n, passes=passes),
        out_shape=jax.ShapeDtypeStruct((n, n), F32),
        in_specs=[pl.BlockSpec(memory_space=pltpu.VMEM)],
        out_specs=pl.BlockSpec(memory_space=pltpu.VMEM),
        scratch_shapes=[pltpu.VMEM((128, 128), F32)],
        compiler_params=pltpu.CompilerParams(vmem_limit_bytes=60 << 20),
        name="chol_inv",
        cost_estimate=pl.CostEstimate(flops=24 * n * n * n, bytes_accessed=8 * n * n, transcendentals=0),
    )(a)


def split2_outside(x):
    hi = lax.reduce_precision(x, 8, 7)
    return hi.astype(BF), lax.reduce_precision(x - hi, 8, 7).astype(BF)


def matern(first_x, first_y, second_x, second_y):
    spacing = 1.0 / GX
    delta_x = (first_x - second_x) * spacing
    delta_y = (first_y - second_y) * spacing
    scaled = jnp.sqrt(3.0) * jnp.sqrt(delta_x * delta_x + delta_y * delta_y) / length_scale
    return (1.0 + scaled) * jnp.exp(-scaled)


def slot_of_tile(slot_tile, tile_count):
    flat_tiles = slot_tile.reshape(-1)
    tiles = jnp.arange(tile_count, dtype=jnp.int32)
    slots = jnp.arange(flat_tiles.shape[0], dtype=jnp.int32)
    return jnp.sum(jnp.where(flat_tiles[None, :] == tiles[:, None], slots[None, :], 0), axis=1)


def shift(x, axis, size, by):
    return lax.ppermute(x, axis, [(i, (i + by) % size) for i in range(size)])


def ring_gather(x, core, cols, rows):
    half = x.shape[0] // 2
    quarter = half // 2
    mine = lax.dynamic_slice_in_dim(x, core * half, half, 0)
    from_prev = shift(mine, "cols", cols, 1)
    from_next = shift(mine, "cols", cols, -1)
    far_a = shift(from_prev[:quarter], "cols", cols, 1)
    far_b = shift(from_next[quarter:], "cols", cols, -1)
    pair = [(i, i ^ 1) for i in range(rows)]
    got = [from_prev, jnp.concatenate([far_a, far_b], axis=0), from_next]
    other = [lax.ppermute(g, "rows", pair) for g in got]
    first = core == 0
    whole = [
        jnp.concatenate([jnp.where(first, g, o), jnp.where(first, o, g)], axis=0)
        for g, o in zip(got, other)
    ]
    return [x] + whole


def per_device(
    slot_tile,
    slot_ranks,
    diag_ranks,
    panel_left_factors,
    panel_v,
    diag_u,
    diag_v,
    panel_points,
    diag_points,
    rhs_diag,
    rhs_rest,
):
    row_devices = lax.axis_size("rows")
    col_devices = lax.axis_size("cols")
    slot_count = panel_left_factors.shape[1]
    tile_order = diag_u.shape[1]
    rank_max = diag_u.shape[2]
    quarter = tile_order // col_devices
    per_peer = quarter // row_devices
    tile_count = rhs_rest.shape[0]
    row_index = lax.axis_index("rows")
    col_index = lax.axis_index("cols")
    core = row_index % 2
    rank_index = jnp.arange(rank_max, dtype=jnp.int32)
    diag_mask = (rank_index < diag_ranks[0]).astype(BF)
    diagonal_left_factor = diag_u[0] * diag_mask[None, :]
    diagonal_right_factor = diag_v[0] * diag_mask[None, :]
    left_all = ring_gather(diagonal_left_factor, core, col_devices, row_devices)
    diag_core = jnp.einsum(
        "br,bq->rq", diagonal_right_factor, diagonal_right_factor, preferred_element_type=F32
    ).astype(BF)
    core_all = ring_gather(diag_core, core, col_devices, row_devices)
    slot_mask = (rank_index[None, :] < slot_ranks[0, :, 0][:, None]).astype(BF)
    slot_left_factor = panel_left_factors[0] * slot_mask[:, None, :]
    slot_right_factor = panel_v[0] * slot_mask[:, None, :]
    inner_product_core = jnp.einsum(
        "gok,oe->gke", slot_right_factor, diagonal_right_factor, preferred_element_type=F32
    ).astype(BF)
    low_rows = jnp.einsum(
        "lgc,lcz->lgz", slot_left_factor, inner_product_core, preferred_element_type=F32
    ).astype(BF)
    left_cat = jnp.concatenate(left_all, axis=1)
    low_cat = jnp.concatenate(
        [jnp.dot(u, c, preferred_element_type=F32).astype(BF) for u, c in zip(left_all, core_all)],
        axis=1,
    )
    centre = diag_points.astype(F32)
    identity = jnp.eye(tile_order, dtype=F32)
    diag_term = lax.dot_general(low_cat, left_cat, (((1,), (1,)), ((), ())), preferred_element_type=F32)
    own_block = matern(centre[0][:, None], centre[1][:, None], centre[0], centre[1])
    diag_system = own_block + nugget * identity - diag_term
    low_parts = []
    for by in range(col_devices):
        target = (col_index + by) % col_devices
        part = lax.dynamic_slice_in_dim(low_rows, target * quarter, quarter, 1)
        low_parts.append(shift(part, "cols", col_devices, by) if by else part)
    half = tile_order // 2
    rhs_mine = lax.dynamic_slice_in_dim(rhs_diag, core * half, half, 0)
    rhs_mine, diag_system = lax.optimization_barrier((rhs_mine, diag_system))
    rhs_got = jnp.stack([shift(rhs_mine, "cols", col_devices, by) for by in range(1, col_devices)])
    inverse = chol_inv(diag_system)
    inverse, low_parts, rhs_got = lax.optimization_barrier((inverse, low_parts, rhs_got))
    rhs_other = lax.ppermute(rhs_got, "rows", [(i, i ^ 1) for i in range(row_devices)])
    rhs_all = [rhs_diag] + [
        jnp.concatenate([jnp.where(core == 0, g, o), jnp.where(core == 0, o, g)], axis=0)
        for g, o in zip(rhs_got, rhs_other)
    ]
    rhs_order = (col_index - jnp.arange(col_devices)) % col_devices
    rhs_stack = jnp.stack(rhs_all)
    rhs_cat = jnp.concatenate([rhs_stack[rhs_order[k]] for k in range(col_devices)], axis=1)
    update_term = jnp.einsum(
        "snr,br->snb", jnp.concatenate(low_parts, axis=2), left_cat, preferred_element_type=F32
    )
    my_tiles = lax.dynamic_slice_in_dim(slot_tile, row_index, 1, 0)[0]
    live_mask = (my_tiles < tile_count).astype(F32)
    coords = panel_points.astype(F32)
    generated = matern(coords[:, 0, :, None], coords[:, 1, :, None], centre[0], centre[1])
    system_rows = live_mask[:, None, None] * (generated - update_term)
    system_rows = system_rows.reshape(slot_count * quarter, tile_order)
    sys_hi, sys_lo = split2_outside(system_rows)
    inv_hi, inv_lo = split2_outside(inverse)
    rhs_hi, rhs_lo = split2_outside(rhs_cat)
    panel_blocks = []
    solution_blocks = []
    step = 256
    for lo in range(0, tile_order, step):
        hi = lo + step
        a_hi, a_lo = sys_hi[:, :hi], sys_lo[:, :hi]
        b_hi, b_lo = inv_hi[lo:hi, :hi], inv_lo[lo:hi, :hi]
        dims = ((1,), (1,))
        panel_blocks.append((mm(a_hi, b_hi, dims) + (mm(a_hi, b_lo, dims) + mm(a_lo, b_hi, dims))).astype(BF))
        dims = ((1,), (0,))
        r_hi, r_lo = rhs_hi[:hi], rhs_lo[:hi]
        solution_blocks.append(mm(b_hi, r_hi, dims) + (mm(b_hi, r_lo, dims) + mm(b_lo, r_hi, dims)))
    panel_factor = jnp.concatenate(panel_blocks, axis=1)
    solution_all = jnp.concatenate(solution_blocks, axis=0)
    width = rhs_diag.shape[1]
    diag_solution = lax.dynamic_slice_in_dim(solution_all, col_index * width, width, 1)
    forward = solution_all.astype(BF)
    product = jnp.dot(panel_factor, forward, preferred_element_type=F32).astype(BF)
    outgoing = product.reshape(slot_count, per_peer, row_devices, forward.shape[1])
    incoming = lax.all_to_all(outgoing, "rows", split_axis=2, concat_axis=2, tiled=True)
    owner_slot = slot_of_tile(slot_tile, tile_count)
    source_row = owner_slot // slot_count
    source_place = owner_slot % slot_count
    step_index = jnp.arange(per_peer, dtype=jnp.int32)
    pick = ((source_place[:, None] * per_peer + step_index[None, :]) * row_devices + source_row[:, None]).reshape(-1)
    picked = jnp.take(incoming.reshape(-1, forward.shape[1]), pick, axis=0)
    rhs_out = rhs_rest - picked.reshape(rhs_rest.shape).astype(F32)
    return (panel_factor.reshape(slot_count, quarter, tile_order), diag_solution, rhs_out)


def solution(mesh):
    return jax.shard_map(
        per_device,
        mesh=mesh,
        in_specs=(
            P(),
            P("rows", None, "cols"),
            P("cols"),
            P("cols", "rows", None, None),
            P("cols", "rows", None, None),
            P("cols", None, None),
            P("cols", None, None),
            P("rows", None, "cols"),
            P(),
            P(None, "cols"),
            P(None, "cols", None, "rows", None),
        ),
        out_specs=(P("rows", "cols", None), P(None, "cols"), P(None, "cols", None, "rows", None)),
        check_vma=False,
    )
```

```python
import functools

import jax
import jax.numpy as jnp
from jax import lax
from jax.experimental import pallas as pl
from jax.experimental.pallas import tpu as pltpu
from jax.sharding import PartitionSpec as P

GX = 1024

length_scale = 0.3
nugget = 1.0
F32 = jnp.float32
BF = jnp.bfloat16
HI = lax.Precision.HIGHEST


def split2(x):
    hi = x.astype(BF)
    lo = (x - hi.astype(F32)).astype(BF)
    return hi, lo


def mm(a, b, dims):
    return lax.dot_general(a, b, (dims, ((), ())), preferred_element_type=F32)


def mm3(a, b, dims):
    ah, al = split2(a)
    bh, bl = split2(b)
    return mm(ah, bh, dims) + (mm(ah, bl, dims) + mm(al, bh, dims))


def factor_block(rows, lin_ref):
    n = len(rows)
    rows = list(rows)
    lane = lax.broadcasted_iota(jnp.int32, (8, 128), 1)
    sub = lax.broadcasted_iota(jnp.int32, (8, 128), 0)
    bs = lambda x, k: jnp.broadcast_to(x[k:k + 1, :], (8, 128))
    for b in range(n):
        inblock = (lane >= 8 * b) & (lane < 8 * b + 8)
        t = rows[b]
        c = [jnp.broadcast_to(t[:, 8 * b + k:8 * b + k + 1], (8, 128)) for k in range(8)]
        tm = jnp.where(inblock, (lane - 8 * b == sub).astype(F32), t)
        y = tm
        scale = jnp.ones((8, 128), F32)
        avec = jnp.ones((8, 128), F32)
        bvec = jnp.zeros((8, 128), F32)
        for k in range(0, 8, 2):
            ck, cl = c[k], c[k + 1]
            pa, pb, pc = bs(ck, k), bs(ck, k + 1), bs(cl, k + 1)
            det = pa * pc - pb * pb
            r = 1.0 / det
            ek = pc * ck - pb * cl
            fk = pa * cl - pb * ck
            wk, wl = ek * r, fk * r
            at_k, at_l = sub == k, sub == k + 1
            scale = jnp.where(at_k, pa, jnp.where(at_l, pa * det, scale))
            avec = jnp.where(at_l, pa, avec)
            bvec = jnp.where(at_l, pb, bvec)
            if k < 6:
                below = sub > k + 1
                y = y - jnp.where(below, wk * bs(y, k) + wl * bs(y, k + 1), 0.0)
            new = list(c)
            for m in range(8):
                if m in (k, k + 1):
                    continue
                g = ck * bs(ek, m) + cl * bs(fk, m)
                v = c[m] - g * r
                new[m] = jnp.where(at_k, bs(wk, m), jnp.where(at_l, bs(wl, m), v))
            new[k] = jnp.where(at_k, -pc * r, jnp.where(at_l, pb * r, wk))
            new[k + 1] = jnp.where(at_k, pb * r, jnp.where(at_l, -pa * r, wl))
            c = new
        if b < n - 1:
            s = [c[m] * bs(tm, m) for m in range(8)]
            s = ((s[0] + s[1]) + (s[2] + s[3])) + ((s[4] + s[5]) + (s[6] + s[7]))
            sk = [bs(s, k) for k in range(8)]
            for i in range(b + 1, n):
                q = [jnp.broadcast_to(rows[i][:, 8 * b + k:8 * b + k + 1], (8, 128)) * sk[k] for k in range(8)]
                q = ((q[0] + q[1]) + (q[2] + q[3])) + ((q[4] + q[5]) + (q[6] + q[7]))
                rows[i] = jnp.where(inblock, 0.0, rows[i]) + q
        yy = avec * y - bvec * pltpu.roll(y, 1, 0)
        res = yy * lax.rsqrt(scale)
        lin_ref[8 * b:8 * b + 8, :] = jnp.where(lane < 8 * b + 8, res, 0.0)


def chol_inv_kernel(a_ref, x_ref, lin_ref, *, n, passes):
    nb = n // 128
    x_ref[...] = a_ref[...]
    dot = mm3 if passes == 3 else functools.partial(lambda a, b, dims: lax.dot_general(a, b, (dims, ((), ())), preferred_element_type=F32, precision=HI))

    def body(p, _):
        off = pl.multiple_of(p * 128, 128)
        rows = [x_ref[pl.ds(pl.multiple_of(off + 8 * b, 8), 8), pl.ds(off, 128)] for b in range(16)]
        factor_block(rows, lin_ref)
        lin = lin_ref[...]
        for q in range(nb):
            @pl.when(p == q)
            def _():
                lo, hi = 128 * q, 128 * (q + 1)
                left = None
                if q < nb - 1:
                    left = dot(x_ref[hi:, lo:hi], lin, ((1,), (1,)))
                    right = dot(lin, x_ref[lo:hi, hi:], ((1,), (0,)))
                    x_ref[lo:hi, hi:] = jnp.zeros((128, n - hi), F32)
                if q > 0:
                    x_ref[lo:hi, :lo] = dot(lin, x_ref[lo:hi, :lo], ((1,), (0,)))
                x_ref[lo:hi, lo:hi] = lin
                if q < nb - 1:
                    x_ref[hi:, hi:] = x_ref[hi:, hi:] - dot(left, right, ((1,), (0,)))
                    if q > 0:
                        x_ref[hi:, :lo] = x_ref[hi:, :lo] - dot(left, x_ref[lo:hi, :lo], ((1,), (0,)))
                    x_ref[hi:, lo:hi] = -dot(left, lin, ((1,), (0,)))
        return 0

    lax.fori_loop(0, nb, body, 0)


def chol_inv(a, passes=3):
    n = a.shape[0]
    return pl.pallas_call(
        functools.partial(chol_inv_kernel, n=n, passes=passes),
        out_shape=jax.ShapeDtypeStruct((n, n), F32),
        in_specs=[pl.BlockSpec(memory_space=pltpu.VMEM)],
        out_specs=pl.BlockSpec(memory_space=pltpu.VMEM),
        scratch_shapes=[pltpu.VMEM((128, 128), F32)],
        compiler_params=pltpu.CompilerParams(vmem_limit_bytes=60 << 20),
        name="chol_inv",
        cost_estimate=pl.CostEstimate(flops=24 * n * n * n, bytes_accessed=8 * n * n, transcendentals=0),
    )(a)


def split2_outside(x):
    hi = lax.reduce_precision(x, 8, 7)
    return hi.astype(BF), lax.reduce_precision(x - hi, 8, 7).astype(BF)


def matern(first_x, first_y, second_x, second_y):
    spacing = 1.0 / GX
    delta_x = (first_x - second_x) * spacing
    delta_y = (first_y - second_y) * spacing
    scaled = jnp.sqrt(3.0) * jnp.sqrt(delta_x * delta_x + delta_y * delta_y) / length_scale
    return (1.0 + scaled) * jnp.exp(-scaled)


MESH = pl.DeviceIdType.MESH


def front_kernel(
    ranks_ref, u_ref, c_ref, left_ref, right_ref, vd_ref, col_ref, row_ref,
    a_ref, low_ref, all_ref,
    ug, cg, send, recv,
):
    n = u_ref.shape[0]
    rows, cols = lax.axis_index("rows"), lax.axis_index("cols")
    count = lax.axis_size("cols")
    core = lax.rem(rows, 2)
    up = {"cols": lax.rem(cols + 1, count)}
    down = {"cols": lax.rem(cols + count - 1, count)}
    pair = {"rows": rows + 1 - 2 * core}

    barrier = pltpu.get_barrier_semaphore()
    for peer in (up, down, pair):
        pl.semaphore_signal(barrier, inc=1, device_id=peer, device_id_type=MESH)
    pl.semaphore_wait(barrier, 3)

    def copy(k, src, dst, peer):
        return pltpu.make_async_remote_copy(
            src_ref=src, dst_ref=dst, send_sem=send.at[k], recv_sem=recv.at[k], device_id=peer, device_id_type=MESH
        )

    def part(ref, lead, start, size):
        sl = pl.ds(pl.multiple_of(start, 64), size)
        return ref.at[sl, :] if lead is None else ref.at[lead, sl, :]

    hu, hc = n // 2, c_ref.shape[0] // 2
    su, sc = core * hu, core * hc
    near = [
        copy(0, part(u_ref, None, su, hu), part(ug, 0, su, hu), up),
        copy(1, part(c_ref, None, sc, hc), part(cg, 0, sc, hc), up),
        copy(2, part(u_ref, None, su, hu), part(ug, 2, su, hu), down),
        copy(3, part(c_ref, None, sc, hc), part(cg, 2, sc, hc), down),
    ]
    qu, qc = hu // 2, hc // 2
    far = [
        copy(4, part(ug, 0, su, qu), part(ug, 1, su, qu), up),
        copy(5, part(cg, 0, sc, qc), part(cg, 1, sc, qc), up),
        copy(6, part(ug, 2, su + qu, qu), part(ug, 1, su + qu, qu), down),
        copy(7, part(cg, 2, sc + qc, qc), part(cg, 1, sc + qc, qc), down),
    ]
    swap = []
    for k, slot in enumerate((0, 2, 1)):
        swap.append(copy(8 + 2 * k, part(ug, slot, su, hu), part(ug, slot, su, hu), pair))
        swap.append(copy(9 + 2 * k, part(cg, slot, sc, hc), part(cg, slot, sc, hc), pair))
    for d in near:
        d.start()

    rank = c_ref.shape[0]
    k_index = lax.broadcasted_iota(jnp.int32, (rank, rank), 0)
    e_index = lax.broadcasted_iota(jnp.int32, (rank, rank), 1)
    for s in range(left_ref.shape[0]):
        keep = (k_index < ranks_ref[s]) & (e_index < ranks_ref[left_ref.shape[0]])
        inner = mm(right_ref[s], vd_ref[...], ((0,), (0,)))
        inner = jnp.where(keep, inner, 0.0).astype(BF)
        low_ref[s] = mm(left_ref[s], inner, ((1,), (0,))).astype(BF)

    for d in near:
        d.wait_recv()
    for d in far:
        d.start()
    for d in swap[:4]:
        d.start()

    step = 64
    line = lax.broadcasted_iota(jnp.int32, (step, n), 1)
    inside = lax.broadcasted_iota(jnp.int32, (step, n), 0)

    def fill(i, _):
        at = pl.ds(pl.multiple_of(i * step, step), step)
        block = matern(col_ref[at, 0:1], col_ref[at, 1:2], row_ref[0:1, :], row_ref[1:2, :])
        a_ref[at, :] = block + jnp.where(line == inside + i * step, nugget, 0.0)
        return 0

    lax.fori_loop(0, n // step // 2, fill, 0)
    for d in far:
        d.wait_recv()
    for d in swap[4:]:
        d.start()
    lax.fori_loop(n // step // 2, n // step, fill, 0)

    def subtract(u, c, where):
        all_ref[:, where * rank:(where + 1) * rank] = u
        wide = 256

        def chunk(i, _):
            at = pl.ds(pl.multiple_of(i * wide, wide), wide)
            low = mm(all_ref[at, where * rank:(where + 1) * rank], c, ((1,), (0,))).astype(BF)
            a_ref[at, :] = a_ref[at, :] - mm(low, u, ((1,), (1,)))
            return 0

        lax.fori_loop(0, n // wide, chunk, 0)

    subtract(u_ref[...], c_ref[...], 0)
    for k, slot in enumerate((0, 2, 1)):
        swap[2 * k].wait_recv()
        swap[2 * k + 1].wait_recv()
        subtract(ug[slot], cg[slot], slot + 1)
    for d in near + far + swap:
        d.wait_send()


def front(ranks, u, c, left, right, vd, col, row):
    n, rank = u.shape
    slots = left.shape[0]
    vmem = pl.BlockSpec(memory_space=pltpu.VMEM)
    return pl.pallas_call(
        front_kernel,
        out_shape=(
            jax.ShapeDtypeStruct((n, n), F32),
            jax.ShapeDtypeStruct((slots, n, rank), BF),
            jax.ShapeDtypeStruct((n, 4 * rank), BF),
        ),
        in_specs=[pl.BlockSpec(memory_space=pltpu.SMEM)] + [vmem] * 7,
        out_specs=(vmem, vmem, vmem),
        scratch_shapes=[
            pltpu.VMEM((3, n, rank), BF),
            pltpu.VMEM((3, rank, rank), BF),
            pltpu.SemaphoreType.DMA((14,)),
            pltpu.SemaphoreType.DMA((14,)),
        ],
        compiler_params=pltpu.CompilerParams(collective_id=0, has_side_effects=True, vmem_limit_bytes=60 << 20),
        name="front",
    )(ranks, u, c, left, right, vd, col, row)


def slot_of_tile(slot_tile, tile_count):
    flat_tiles = slot_tile.reshape(-1)
    tiles = jnp.arange(tile_count, dtype=jnp.int32)
    slots = jnp.arange(flat_tiles.shape[0], dtype=jnp.int32)
    return jnp.sum(jnp.where(flat_tiles[None, :] == tiles[:, None], slots[None, :], 0), axis=1)


def shift(x, axis, size, by):
    return lax.ppermute(x, axis, [(i, (i + by) % size) for i in range(size)])


def per_device(
    slot_tile,
    slot_ranks,
    diag_ranks,
    panel_left_factors,
    panel_v,
    diag_u,
    diag_v,
    panel_points,
    diag_points,
    rhs_diag,
    rhs_rest,
):
    row_devices = lax.axis_size("rows")
    col_devices = lax.axis_size("cols")
    slot_count = panel_left_factors.shape[1]
    tile_order = diag_u.shape[1]
    rank_max = diag_u.shape[2]
    quarter = tile_order // col_devices
    per_peer = quarter // row_devices
    tile_count = rhs_rest.shape[0]
    row_index = lax.axis_index("rows")
    col_index = lax.axis_index("cols")
    core = row_index % 2
    rank_index = jnp.arange(rank_max, dtype=jnp.int32)
    diag_mask = (rank_index < diag_ranks[0]).astype(BF)
    diagonal_right_factor = diag_v[0] * diag_mask[None, :]
    diag_core = jnp.einsum(
        "br,bq->rq", diagonal_right_factor, diagonal_right_factor, preferred_element_type=F32
    ).astype(BF)
    ranks = jnp.concatenate([slot_ranks[0, :, 0], diag_ranks])
    centre = diag_points.astype(F32)
    diag_system, low_rows, left_cat = front(
        ranks, diag_u[0], diag_core, panel_left_factors[0], panel_v[0], diag_v[0], centre.T, centre
    )
    low_parts = []
    for by in range(col_devices):
        target = (col_index + by) % col_devices
        part = lax.dynamic_slice_in_dim(low_rows, target * quarter, quarter, 1)
        low_parts.append(shift(part, "cols", col_devices, by) if by else part)
    half = tile_order // 2
    rhs_mine = lax.dynamic_slice_in_dim(rhs_diag, core * half, half, 0)
    rhs_mine, diag_system = lax.optimization_barrier((rhs_mine, diag_system))
    rhs_got = jnp.stack([shift(rhs_mine, "cols", col_devices, by) for by in range(1, col_devices)])
    inverse = chol_inv(diag_system)
    inverse, low_parts, rhs_got = lax.optimization_barrier((inverse, low_parts, rhs_got))
    rhs_other = lax.ppermute(rhs_got, "rows", [(i, i ^ 1) for i in range(row_devices)])
    rhs_all = [rhs_diag] + [
        jnp.concatenate([jnp.where(core == 0, g, o), jnp.where(core == 0, o, g)], axis=0)
        for g, o in zip(rhs_got, rhs_other)
    ]
    rhs_order = (col_index - jnp.arange(col_devices)) % col_devices
    rhs_stack = jnp.stack(rhs_all)
    rhs_cat = jnp.concatenate([rhs_stack[rhs_order[k]] for k in range(col_devices)], axis=1)
    update_term = jnp.einsum(
        "snr,br->snb", jnp.concatenate(low_parts, axis=2), left_cat, preferred_element_type=F32
    )
    my_tiles = lax.dynamic_slice_in_dim(slot_tile, row_index, 1, 0)[0]
    live_mask = (my_tiles < tile_count).astype(F32)
    coords = panel_points.astype(F32)
    generated = matern(coords[:, 0, :, None], coords[:, 1, :, None], centre[0], centre[1])
    system_rows = live_mask[:, None, None] * (generated - update_term)
    system_rows = system_rows.reshape(slot_count * quarter, tile_order)
    sys_hi, sys_lo = split2_outside(system_rows)
    inv_hi, inv_lo = split2_outside(inverse)
    rhs_hi, rhs_lo = split2_outside(rhs_cat)
    panel_blocks = []
    solution_blocks = []
    step = 256
    for lo in range(0, tile_order, step):
        hi = lo + step
        a_hi, a_lo = sys_hi[:, :hi], sys_lo[:, :hi]
        b_hi, b_lo = inv_hi[lo:hi, :hi], inv_lo[lo:hi, :hi]
        dims = ((1,), (1,))
        panel_blocks.append((mm(a_hi, b_hi, dims) + (mm(a_hi, b_lo, dims) + mm(a_lo, b_hi, dims))).astype(BF))
        dims = ((1,), (0,))
        r_hi, r_lo = rhs_hi[:hi], rhs_lo[:hi]
        solution_blocks.append(mm(b_hi, r_hi, dims) + (mm(b_hi, r_lo, dims) + mm(b_lo, r_hi, dims)))
    panel_factor = jnp.concatenate(panel_blocks, axis=1)
    solution_all = jnp.concatenate(solution_blocks, axis=0)
    width = rhs_diag.shape[1]
    diag_solution = lax.dynamic_slice_in_dim(solution_all, col_index * width, width, 1)
    forward = solution_all.astype(BF)
    product = jnp.dot(panel_factor, forward, preferred_element_type=F32).astype(BF)
    outgoing = product.reshape(slot_count, per_peer, row_devices, forward.shape[1])
    incoming = lax.all_to_all(outgoing, "rows", split_axis=2, concat_axis=2, tiled=True)
    owner_slot = slot_of_tile(slot_tile, tile_count)
    source_row = owner_slot // slot_count
    source_place = owner_slot % slot_count
    step_index = jnp.arange(per_peer, dtype=jnp.int32)
    pick = ((source_place[:, None] * per_peer + step_index[None, :]) * row_devices + source_row[:, None]).reshape(-1)
    picked = jnp.take(incoming.reshape(-1, forward.shape[1]), pick, axis=0)
    rhs_out = rhs_rest - picked.reshape(rhs_rest.shape).astype(F32)
    return (panel_factor.reshape(slot_count, quarter, tile_order), diag_solution, rhs_out)


def solution(mesh):
    return jax.shard_map(
        per_device,
        mesh=mesh,
        in_specs=(
            P(),
            P("rows", None, "cols"),
            P("cols"),
            P("cols", "rows", None, None),
            P("cols", "rows", None, None),
            P("cols", None, None),
            P("cols", None, None),
            P("rows", None, "cols"),
            P(),
            P(None, "cols"),
            P(None, "cols", None, "rows", None),
        ),
        out_specs=(P("rows", "cols", None), P(None, "cols"), P(None, "cols", None, "rows", None)),
        check_vma=False,
    )
```

```python
import functools

import jax
import jax.numpy as jnp
from jax import lax
from jax.experimental import pallas as pl
from jax.experimental.pallas import tpu as pltpu
from jax.sharding import PartitionSpec as P

GX = 1024

length_scale = 0.3
nugget = 1.0
F32 = jnp.float32
BF = jnp.bfloat16
HI = lax.Precision.HIGHEST


def split2(x):
    hi = x.astype(BF)
    lo = (x - hi.astype(F32)).astype(BF)
    return hi, lo


def mm(a, b, dims):
    return lax.dot_general(a, b, (dims, ((), ())), preferred_element_type=F32)


def mm3(a, b, dims):
    ah, al = split2(a)
    bh, bl = split2(b)
    return mm(ah, bh, dims) + (mm(ah, bl, dims) + mm(al, bh, dims))


def factor_block(rows, lin_ref):
    n = len(rows)
    rows = list(rows)
    lane = lax.broadcasted_iota(jnp.int32, (8, 128), 1)
    sub = lax.broadcasted_iota(jnp.int32, (8, 128), 0)
    bs = lambda x, k: jnp.broadcast_to(x[k:k + 1, :], (8, 128))
    for b in range(n):
        inblock = (lane >= 8 * b) & (lane < 8 * b + 8)
        t = rows[b]
        c = [jnp.broadcast_to(t[:, 8 * b + k:8 * b + k + 1], (8, 128)) for k in range(8)]
        tm = jnp.where(inblock, (lane - 8 * b == sub).astype(F32), t)
        y = tm
        scale = jnp.ones((8, 128), F32)
        avec = jnp.ones((8, 128), F32)
        bvec = jnp.zeros((8, 128), F32)
        for k in range(0, 8, 2):
            ck, cl = c[k], c[k + 1]
            pa, pb, pc = bs(ck, k), bs(ck, k + 1), bs(cl, k + 1)
            det = pa * pc - pb * pb
            r = 1.0 / det
            ek = pc * ck - pb * cl
            fk = pa * cl - pb * ck
            wk, wl = ek * r, fk * r
            at_k, at_l = sub == k, sub == k + 1
            scale = jnp.where(at_k, pa, jnp.where(at_l, pa * det, scale))
            avec = jnp.where(at_l, pa, avec)
            bvec = jnp.where(at_l, pb, bvec)
            if k < 6:
                below = sub > k + 1
                y = y - jnp.where(below, wk * bs(y, k) + wl * bs(y, k + 1), 0.0)
            new = list(c)
            for m in range(8):
                if m in (k, k + 1):
                    continue
                g = ck * bs(ek, m) + cl * bs(fk, m)
                v = c[m] - g * r
                new[m] = jnp.where(at_k, bs(wk, m), jnp.where(at_l, bs(wl, m), v))
            new[k] = jnp.where(at_k, -pc * r, jnp.where(at_l, pb * r, wk))
            new[k + 1] = jnp.where(at_k, pb * r, jnp.where(at_l, -pa * r, wl))
            c = new
        if b < n - 1:
            s = [c[m] * bs(tm, m) for m in range(8)]
            s = ((s[0] + s[1]) + (s[2] + s[3])) + ((s[4] + s[5]) + (s[6] + s[7]))
            sk = [bs(s, k) for k in range(8)]
            for i in range(b + 1, n):
                q = [jnp.broadcast_to(rows[i][:, 8 * b + k:8 * b + k + 1], (8, 128)) * sk[k] for k in range(8)]
                q = ((q[0] + q[1]) + (q[2] + q[3])) + ((q[4] + q[5]) + (q[6] + q[7]))
                rows[i] = jnp.where(inblock, 0.0, rows[i]) + q
        yy = avec * y - bvec * pltpu.roll(y, 1, 0)
        res = yy * lax.rsqrt(scale)
        lin_ref[8 * b:8 * b + 8, :] = jnp.where(lane < 8 * b + 8, res, 0.0)


def chol_inv_kernel(a_ref, x_ref, lin_ref, *, n, passes):
    nb = n // 128
    x_ref[...] = a_ref[...]
    dot = mm3 if passes == 3 else functools.partial(lambda a, b, dims: lax.dot_general(a, b, (dims, ((), ())), preferred_element_type=F32, precision=HI))

    def body(p, _):
        off = pl.multiple_of(p * 128, 128)
        rows = [x_ref[pl.ds(pl.multiple_of(off + 8 * b, 8), 8), pl.ds(off, 128)] for b in range(16)]
        factor_block(rows, lin_ref)
        lin = lin_ref[...]
        for q in range(nb):
            @pl.when(p == q)
            def _():
                lo, hi = 128 * q, 128 * (q + 1)
                left = None
                if q < nb - 1:
                    left = dot(x_ref[hi:, lo:hi], lin, ((1,), (1,)))
                    right = dot(lin, x_ref[lo:hi, hi:], ((1,), (0,)))
                    x_ref[lo:hi, hi:] = jnp.zeros((128, n - hi), F32)
                if q > 0:
                    x_ref[lo:hi, :lo] = dot(lin, x_ref[lo:hi, :lo], ((1,), (0,)))
                x_ref[lo:hi, lo:hi] = lin
                if q < nb - 1:
                    x_ref[hi:, hi:] = x_ref[hi:, hi:] - dot(left, right, ((1,), (0,)))
                    if q > 0:
                        x_ref[hi:, :lo] = x_ref[hi:, :lo] - dot(left, x_ref[lo:hi, :lo], ((1,), (0,)))
                    x_ref[hi:, lo:hi] = -dot(left, lin, ((1,), (0,)))
        return 0

    lax.fori_loop(0, nb, body, 0)


def chol_inv(a, passes=3):
    n = a.shape[0]
    return pl.pallas_call(
        functools.partial(chol_inv_kernel, n=n, passes=passes),
        out_shape=jax.ShapeDtypeStruct((n, n), F32),
        in_specs=[pl.BlockSpec(memory_space=pltpu.VMEM)],
        out_specs=pl.BlockSpec(memory_space=pltpu.VMEM),
        scratch_shapes=[pltpu.VMEM((128, 128), F32)],
        compiler_params=pltpu.CompilerParams(vmem_limit_bytes=60 << 20),
        name="chol_inv",
        cost_estimate=pl.CostEstimate(flops=24 * n * n * n, bytes_accessed=8 * n * n, transcendentals=0),
    )(a)


def split2_outside(x):
    hi = lax.reduce_precision(x, 8, 7)
    return hi.astype(BF), lax.reduce_precision(x - hi, 8, 7).astype(BF)


def matern(first_x, first_y, second_x, second_y):
    spacing = 1.0 / GX
    delta_x = (first_x - second_x) * spacing
    delta_y = (first_y - second_y) * spacing
    scaled = jnp.sqrt(3.0) * jnp.sqrt(delta_x * delta_x + delta_y * delta_y) / length_scale
    return (1.0 + scaled) * jnp.exp(-scaled)


MESH = pl.DeviceIdType.MESH


def front_kernel(
    ranks_ref, u_ref, c_ref, left_ref, right_ref, vd_ref, col_ref, row_ref,
    a_ref, got_ref, all_ref,
    ug, cg, low_ref, via_up, via_down, send, recv,
):
    n = u_ref.shape[0]
    rows, cols = lax.axis_index("rows"), lax.axis_index("cols")
    count = lax.axis_size("cols")
    core = lax.rem(rows, 2)
    up = {"cols": lax.rem(cols + 1, count)}
    down = {"cols": lax.rem(cols + count - 1, count)}
    pair = {"rows": rows + 1 - 2 * core}

    barrier = pltpu.get_barrier_semaphore()
    for peer in (up, down, pair):
        pl.semaphore_signal(barrier, inc=1, device_id=peer, device_id_type=MESH)
    pl.semaphore_wait(barrier, 3)

    def copy(k, src, dst, peer):
        return pltpu.make_async_remote_copy(
            src_ref=src, dst_ref=dst, send_sem=send.at[k], recv_sem=recv.at[k], device_id=peer, device_id_type=MESH
        )

    def part(ref, lead, start, size):
        sl = pl.ds(pl.multiple_of(start, 64), size)
        return ref.at[sl, :] if lead is None else ref.at[lead, sl, :]

    hu, hc = n // 2, c_ref.shape[0] // 2
    su, sc = core * hu, core * hc
    near = [
        copy(0, part(u_ref, None, su, hu), part(ug, 0, su, hu), up),
        copy(1, part(c_ref, None, sc, hc), part(cg, 0, sc, hc), up),
        copy(2, part(u_ref, None, su, hu), part(ug, 2, su, hu), down),
        copy(3, part(c_ref, None, sc, hc), part(cg, 2, sc, hc), down),
    ]
    qu, qc = hu // 2, hc // 2
    far = [
        copy(4, part(ug, 0, su, qu), part(ug, 1, su, qu), up),
        copy(5, part(cg, 0, sc, qc), part(cg, 1, sc, qc), up),
        copy(6, part(ug, 2, su + qu, qu), part(ug, 1, su + qu, qu), down),
        copy(7, part(cg, 2, sc + qc, qc), part(cg, 1, sc + qc, qc), down),
    ]
    swap = []
    for k, slot in enumerate((0, 2, 1)):
        swap.append(copy(8 + 2 * k, part(ug, slot, su, hu), part(ug, slot, su, hu), pair))
        swap.append(copy(9 + 2 * k, part(cg, slot, sc, hc), part(cg, slot, sc, hc), pair))
    quarter = got_ref.shape[1]
    middle = quarter // 2

    def lows(by, start, size):
        target = lax.rem(cols + by, count)
        return low_ref.at[:, pl.ds(pl.multiple_of(target * quarter + start, middle), size), :]

    def into(by, start, size):
        width = low_ref.shape[2]
        return got_ref.at[:, pl.ds(start, size), pl.ds(by * width, width)]

    relay = [copy(14, lows(2, 0, middle), via_up, up), copy(15, lows(2, middle, middle), via_down, down)]
    direct = [copy(16, lows(1, 0, quarter), into(1, 0, quarter), up), copy(17, lows(3, 0, quarter), into(3, 0, quarter), down)]
    onward = [copy(18, via_up, into(2, 0, middle), up), copy(19, via_down, into(2, middle, middle), down)]
    for d in near:
        d.start()

    rank = c_ref.shape[0]
    k_index = lax.broadcasted_iota(jnp.int32, (rank, rank), 0)
    e_index = lax.broadcasted_iota(jnp.int32, (rank, rank), 1)
    for s in range(left_ref.shape[0]):
        keep = (k_index < ranks_ref[s]) & (e_index < ranks_ref[left_ref.shape[0]])
        inner = mm(right_ref[s], vd_ref[...], ((0,), (0,)))
        inner = jnp.where(keep, inner, 0.0).astype(BF)
        low_ref[s] = mm(left_ref[s], inner, ((1,), (0,))).astype(BF)

    for d in near:
        d.wait_recv()
    for d in far:
        d.start()
    for d in swap[:4]:
        d.start()
    for d in relay + direct:
        d.start()
    got_ref[:, :, 0:rank] = low_ref[:, pl.ds(pl.multiple_of(cols * quarter, quarter), quarter), :]

    step = 32
    line = lax.broadcasted_iota(jnp.int32, (step, n), 1)
    inside = lax.broadcasted_iota(jnp.int32, (step, n), 0)

    def fill(i, _):
        at = pl.ds(pl.multiple_of(i * step, step), step)
        block = matern(col_ref[at, 0:1], col_ref[at, 1:2], row_ref[0:1, :], row_ref[1:2, :])
        a_ref[at, :] = block + jnp.where(line == inside + i * step, nugget, 0.0)
        return 0

    lax.fori_loop(0, n // step // 2, fill, 0)
    for d in far:
        d.wait_recv()
    for d in swap[4:]:
        d.start()
    lax.fori_loop(n // step // 2, n // step, fill, 0)

    def subtract(u, c, where):
        all_ref[:, where * rank:(where + 1) * rank] = u
        wide = 256

        def chunk(i, _):
            at = pl.ds(pl.multiple_of(i * wide, wide), wide)
            low = mm(all_ref[at, where * rank:(where + 1) * rank], c, ((1,), (0,))).astype(BF)
            a_ref[at, :] = a_ref[at, :] - mm(low, u, ((1,), (1,)))
            return 0

        lax.fori_loop(0, n // wide, chunk, 0)

    subtract(u_ref[...], c_ref[...], 0)
    for d in relay:
        d.wait_recv()
    for d in onward:
        d.start()
    for k, slot in enumerate((0, 2, 1)):
        swap[2 * k].wait_recv()
        swap[2 * k + 1].wait_recv()
        subtract(ug[slot], cg[slot], slot + 1)
    for d in direct + onward:
        d.wait_recv()
    for d in near + far + swap + relay + direct + onward:
        d.wait_send()


def front(ranks, u, c, left, right, vd, col, row):
    n, rank = u.shape
    slots = left.shape[0]
    vmem = pl.BlockSpec(memory_space=pltpu.VMEM)
    return pl.pallas_call(
        front_kernel,
        out_shape=(
            jax.ShapeDtypeStruct((n, n), F32),
            jax.ShapeDtypeStruct((slots, n // 4, 4 * rank), BF),
            jax.ShapeDtypeStruct((n, 4 * rank), BF),
        ),
        in_specs=[pl.BlockSpec(memory_space=pltpu.SMEM)] + [vmem] * 7,
        out_specs=(vmem, vmem, vmem),
        scratch_shapes=[
            pltpu.VMEM((3, n, rank), BF),
            pltpu.VMEM((3, rank, rank), BF),
            pltpu.VMEM((slots, n, rank), BF),
            pltpu.VMEM((slots, n // 8, rank), BF),
            pltpu.VMEM((slots, n // 8, rank), BF),
            pltpu.SemaphoreType.DMA((20,)),
            pltpu.SemaphoreType.DMA((20,)),
        ],
        compiler_params=pltpu.CompilerParams(collective_id=0, has_side_effects=True, vmem_limit_bytes=60 << 20),
        name="front",
    )(ranks, u, c, left, right, vd, col, row)


def exchange_kernel(x_ref, o_ref, send, recv, own):
    me, count = lax.axis_index("rows"), lax.axis_size("rows")
    barrier = pltpu.get_barrier_semaphore()

    def greet(i, _):
        pl.semaphore_signal(
            barrier, inc=1, device_id={"rows": lax.rem(me + i, count)}, device_id_type=MESH
        )
        return 0

    lax.fori_loop(1, count, greet, 0)
    keep = pltpu.make_async_copy(x_ref.at[me], o_ref.at[me], own)
    keep.start()
    pl.semaphore_wait(barrier, count - 1)

    def copy(i):
        peer = lax.rem(me + i, count)
        return pltpu.make_async_remote_copy(
            src_ref=x_ref.at[peer], dst_ref=o_ref.at[me], send_sem=send.at[i], recv_sem=recv.at[i],
            device_id={"rows": peer}, device_id_type=MESH,
        )

    def start(i, _):
        copy(i).start()
        return 0

    def finish(i, _):
        copy(i).wait()
        return 0

    lax.fori_loop(1, count, start, 0)
    keep.wait()
    lax.fori_loop(1, count, finish, 0)


def exchange(x):
    vmem = pl.BlockSpec(memory_space=pltpu.VMEM)
    return pl.pallas_call(
        exchange_kernel,
        out_shape=jax.ShapeDtypeStruct(x.shape, x.dtype),
        in_specs=[vmem],
        out_specs=vmem,
        scratch_shapes=[
            pltpu.SemaphoreType.DMA((x.shape[0],)),
            pltpu.SemaphoreType.DMA((x.shape[0],)),
            pltpu.SemaphoreType.DMA,
        ],
        compiler_params=pltpu.CompilerParams(collective_id=1, has_side_effects=True),
        name="exchange",
    )(x)


def slot_of_tile(slot_tile, tile_count):
    flat_tiles = slot_tile.reshape(-1)
    tiles = jnp.arange(tile_count, dtype=jnp.int32)
    slots = jnp.arange(flat_tiles.shape[0], dtype=jnp.int32)
    return jnp.sum(jnp.where(flat_tiles[None, :] == tiles[:, None], slots[None, :], 0), axis=1)


def shift(x, axis, size, by):
    return lax.ppermute(x, axis, [(i, (i + by) % size) for i in range(size)])


def per_device(
    slot_tile,
    slot_ranks,
    diag_ranks,
    panel_left_factors,
    panel_v,
    diag_u,
    diag_v,
    panel_points,
    diag_points,
    rhs_diag,
    rhs_rest,
):
    row_devices = lax.axis_size("rows")
    col_devices = lax.axis_size("cols")
    slot_count = panel_left_factors.shape[1]
    tile_order = diag_u.shape[1]
    rank_max = diag_u.shape[2]
    quarter = tile_order // col_devices
    per_peer = quarter // row_devices
    tile_count = rhs_rest.shape[0]
    row_index = lax.axis_index("rows")
    col_index = lax.axis_index("cols")
    core = row_index % 2
    rank_index = jnp.arange(rank_max, dtype=jnp.int32)
    diag_mask = (rank_index < diag_ranks[0]).astype(BF)
    diagonal_right_factor = diag_v[0] * diag_mask[None, :]
    diag_core = jnp.einsum(
        "br,bq->rq", diagonal_right_factor, diagonal_right_factor, preferred_element_type=F32
    ).astype(BF)
    ranks = jnp.concatenate([slot_ranks[0, :, 0], diag_ranks])
    centre = diag_points.astype(F32)
    diag_system, low_cat, left_cat = front(
        ranks, diag_u[0], diag_core, panel_left_factors[0], panel_v[0], diag_v[0], centre.T, centre
    )
    half = tile_order // 2
    rhs_mine = lax.dynamic_slice_in_dim(rhs_diag, core * half, half, 0)
    rhs_mine, diag_system = lax.optimization_barrier((rhs_mine, diag_system))
    rhs_got = jnp.stack([shift(rhs_mine, "cols", col_devices, by) for by in range(1, col_devices)])
    inverse = chol_inv(diag_system)
    inverse, rhs_got = lax.optimization_barrier((inverse, rhs_got))
    rhs_other = lax.ppermute(rhs_got, "rows", [(i, i ^ 1) for i in range(row_devices)])
    rhs_all = [rhs_diag] + [
        jnp.concatenate([jnp.where(core == 0, g, o), jnp.where(core == 0, o, g)], axis=0)
        for g, o in zip(rhs_got, rhs_other)
    ]
    rhs_order = (col_index - jnp.arange(col_devices)) % col_devices
    rhs_stack = jnp.stack(rhs_all)
    rhs_cat = jnp.concatenate([rhs_stack[rhs_order[k]] for k in range(col_devices)], axis=1)
    update_term = jnp.einsum(
        "snr,br->snb", low_cat, left_cat, preferred_element_type=F32
    )
    my_tiles = lax.dynamic_slice_in_dim(slot_tile, row_index, 1, 0)[0]
    live_mask = (my_tiles < tile_count).astype(F32)
    coords = panel_points.astype(F32)
    generated = matern(coords[:, 0, :, None], coords[:, 1, :, None], centre[0], centre[1])
    system_rows = live_mask[:, None, None] * (generated - update_term)
    system_rows = system_rows.reshape(slot_count * quarter, tile_order)
    sys_hi, sys_lo = split2_outside(system_rows)
    inv_hi, inv_lo = split2_outside(inverse)
    rhs_hi, rhs_lo = split2_outside(rhs_cat)
    panel_blocks = []
    solution_blocks = []
    step = 256
    for lo in range(0, tile_order, step):
        hi = lo + step
        a_hi, a_lo = sys_hi[:, :hi], sys_lo[:, :hi]
        b_hi, b_lo = inv_hi[lo:hi, :hi], inv_lo[lo:hi, :hi]
        dims = ((1,), (1,))
        panel_blocks.append((mm(a_hi, b_hi, dims) + (mm(a_hi, b_lo, dims) + mm(a_lo, b_hi, dims))).astype(BF))
        dims = ((1,), (0,))
        r_hi, r_lo = rhs_hi[:hi], rhs_lo[:hi]
        solution_blocks.append(mm(b_hi, r_hi, dims) + (mm(b_hi, r_lo, dims) + mm(b_lo, r_hi, dims)))
    panel_factor = jnp.concatenate(panel_blocks, axis=1)
    solution_all = jnp.concatenate(solution_blocks, axis=0)
    width = rhs_diag.shape[1]
    diag_solution = lax.dynamic_slice_in_dim(solution_all, col_index * width, width, 1)
    forward = solution_all.astype(BF)
    product = jnp.dot(panel_factor, forward, preferred_element_type=F32).astype(BF)
    columns = forward.shape[1]
    outgoing = product.reshape(slot_count, per_peer, row_devices, columns).transpose(2, 0, 1, 3)
    incoming = exchange(outgoing.reshape(row_devices, 8, -1))
    owner_slot = slot_of_tile(slot_tile, tile_count)
    picked = jnp.take(incoming.reshape(row_devices * slot_count, per_peer * columns), owner_slot, axis=0)
    rhs_out = rhs_rest - picked.reshape(rhs_rest.shape).astype(F32)
    return (panel_factor.reshape(slot_count, quarter, tile_order), diag_solution, rhs_out)


def solution(mesh):
    return jax.shard_map(
        per_device,
        mesh=mesh,
        in_specs=(
            P(),
            P("rows", None, "cols"),
            P("cols"),
            P("cols", "rows", None, None),
            P("cols", "rows", None, None),
            P("cols", None, None),
            P("cols", None, None),
            P("rows", None, "cols"),
            P(),
            P(None, "cols"),
            P(None, "cols", None, "rows", None),
        ),
        out_specs=(P("rows", "cols", None), P(None, "cols"), P(None, "cols", None, "rows", None)),
        check_vma=False,
    )
```

```python
import functools

import jax
import jax.numpy as jnp
from jax import lax
from jax.experimental import pallas as pl
from jax.experimental.pallas import tpu as pltpu
from jax.sharding import PartitionSpec as P

GX = 1024

length_scale = 0.3
nugget = 1.0
F32 = jnp.float32
BF = jnp.bfloat16
HI = lax.Precision.HIGHEST


def split2(x):
    hi = x.astype(BF)
    lo = (x - hi.astype(F32)).astype(BF)
    return hi, lo


def mm(a, b, dims):
    return lax.dot_general(a, b, (dims, ((), ())), preferred_element_type=F32)


def mm3(a, b, dims):
    ah, al = split2(a)
    bh, bl = split2(b)
    return mm(ah, bh, dims) + (mm(ah, bl, dims) + mm(al, bh, dims))


def factor_block(rows, lin_ref):
    n = len(rows)
    rows = list(rows)
    lane = lax.broadcasted_iota(jnp.int32, (8, 128), 1)
    sub = lax.broadcasted_iota(jnp.int32, (8, 128), 0)
    bs = lambda x, k: jnp.broadcast_to(x[k:k + 1, :], (8, 128))
    for b in range(n):
        inblock = (lane >= 8 * b) & (lane < 8 * b + 8)
        t = rows[b]
        c = [jnp.broadcast_to(t[:, 8 * b + k:8 * b + k + 1], (8, 128)) for k in range(8)]
        tm = jnp.where(inblock, (lane - 8 * b == sub).astype(F32), t)
        y = tm
        scale = jnp.ones((8, 128), F32)
        avec = jnp.ones((8, 128), F32)
        bvec = jnp.zeros((8, 128), F32)
        for k in range(0, 8, 2):
            ck, cl = c[k], c[k + 1]
            pa, pb, pc = bs(ck, k), bs(ck, k + 1), bs(cl, k + 1)
            det = pa * pc - pb * pb
            r = 1.0 / det
            ek = pc * ck - pb * cl
            fk = pa * cl - pb * ck
            wk, wl = ek * r, fk * r
            at_k, at_l = sub == k, sub == k + 1
            scale = jnp.where(at_k, pa, jnp.where(at_l, pa * det, scale))
            avec = jnp.where(at_l, pa, avec)
            bvec = jnp.where(at_l, pb, bvec)
            if k < 6:
                below = sub > k + 1
                y = y - jnp.where(below, wk * bs(y, k) + wl * bs(y, k + 1), 0.0)
            new = list(c)
            for m in range(8):
                if m in (k, k + 1):
                    continue
                g = ck * bs(ek, m) + cl * bs(fk, m)
                v = c[m] - g * r
                new[m] = jnp.where(at_k, bs(wk, m), jnp.where(at_l, bs(wl, m), v))
            new[k] = jnp.where(at_k, -pc * r, jnp.where(at_l, pb * r, wk))
            new[k + 1] = jnp.where(at_k, pb * r, jnp.where(at_l, -pa * r, wl))
            c = new
        if b < n - 1:
            s = [c[m] * bs(tm, m) for m in range(8)]
            s = ((s[0] + s[1]) + (s[2] + s[3])) + ((s[4] + s[5]) + (s[6] + s[7]))
            sk = [bs(s, k) for k in range(8)]
            for i in range(b + 1, n):
                q = [jnp.broadcast_to(rows[i][:, 8 * b + k:8 * b + k + 1], (8, 128)) * sk[k] for k in range(8)]
                q = ((q[0] + q[1]) + (q[2] + q[3])) + ((q[4] + q[5]) + (q[6] + q[7]))
                rows[i] = jnp.where(inblock, 0.0, rows[i]) + q
        yy = avec * y - bvec * pltpu.roll(y, 1, 0)
        res = yy * lax.rsqrt(scale)
        lin_ref[8 * b:8 * b + 8, :] = jnp.where(lane < 8 * b + 8, res, 0.0)


def chol_inv_kernel(a_ref, x_ref, lin_ref, *, n, passes):
    nb = n // 128
    x_ref[...] = a_ref[...]
    dot = mm3 if passes == 3 else functools.partial(lambda a, b, dims: lax.dot_general(a, b, (dims, ((), ())), preferred_element_type=F32, precision=HI))

    def body(p, _):
        off = pl.multiple_of(p * 128, 128)
        rows = [x_ref[pl.ds(pl.multiple_of(off + 8 * b, 8), 8), pl.ds(off, 128)] for b in range(16)]
        factor_block(rows, lin_ref)
        lin = lin_ref[...]
        for q in range(nb):
            @pl.when(p == q)
            def _():
                lo, hi = 128 * q, 128 * (q + 1)
                left = None
                if q < nb - 1:
                    left = dot(x_ref[hi:, lo:hi], lin, ((1,), (1,)))
                    right = dot(lin, x_ref[lo:hi, hi:], ((1,), (0,)))
                    x_ref[lo:hi, hi:] = jnp.zeros((128, n - hi), F32)
                if q > 0:
                    x_ref[lo:hi, :lo] = dot(lin, x_ref[lo:hi, :lo], ((1,), (0,)))
                x_ref[lo:hi, lo:hi] = lin
                if q < nb - 1:
                    x_ref[hi:, hi:] = x_ref[hi:, hi:] - dot(left, right, ((1,), (0,)))
                    if q > 0:
                        x_ref[hi:, :lo] = x_ref[hi:, :lo] - dot(left, x_ref[lo:hi, :lo], ((1,), (0,)))
                    x_ref[hi:, lo:hi] = -dot(left, lin, ((1,), (0,)))
        return 0

    lax.fori_loop(0, nb, body, 0)


def chol_inv(a, passes=3):
    n = a.shape[0]
    return pl.pallas_call(
        functools.partial(chol_inv_kernel, n=n, passes=passes),
        out_shape=jax.ShapeDtypeStruct((n, n), F32),
        in_specs=[pl.BlockSpec(memory_space=pltpu.VMEM)],
        out_specs=pl.BlockSpec(memory_space=pltpu.VMEM),
        scratch_shapes=[pltpu.VMEM((128, 128), F32)],
        compiler_params=pltpu.CompilerParams(vmem_limit_bytes=60 << 20),
        name="chol_inv",
        cost_estimate=pl.CostEstimate(flops=24 * n * n * n, bytes_accessed=8 * n * n, transcendentals=0),
    )(a)


def split2_outside(x):
    hi = lax.reduce_precision(x, 8, 7)
    return hi.astype(BF), lax.reduce_precision(x - hi, 8, 7).astype(BF)


def matern(first_x, first_y, second_x, second_y):
    delta_x = first_x - second_x
    delta_y = first_y - second_y
    scaled = jnp.sqrt(delta_x * delta_x + delta_y * delta_y) * (3.0**0.5 / (GX * length_scale))
    return (1.0 + scaled) * jnp.exp(-scaled)


MESH = pl.DeviceIdType.MESH


def front_kernel(
    ranks_ref, diag_rank_ref, u_ref, c_ref, left_ref, right_ref, vd_ref, col_ref, row_ref,
    a_ref, low_ref, all_ref,
    ug, cg, send, recv,
):
    n = u_ref.shape[0]
    rows, cols = lax.axis_index("rows"), lax.axis_index("cols")
    count = lax.axis_size("cols")
    core = lax.rem(rows, 2)
    up = {"cols": lax.rem(cols + 1, count)}
    down = {"cols": lax.rem(cols + count - 1, count)}
    pair = {"rows": rows + 1 - 2 * core}

    barrier = pltpu.get_barrier_semaphore()
    for peer in (up, down, pair):
        pl.semaphore_signal(barrier, inc=1, device_id=peer, device_id_type=MESH)
    pl.semaphore_wait(barrier, 3)

    def copy(k, src, dst, peer):
        return pltpu.make_async_remote_copy(
            src_ref=src, dst_ref=dst, send_sem=send.at[k], recv_sem=recv.at[k], device_id=peer, device_id_type=MESH
        )

    def part(ref, lead, start, size):
        sl = pl.ds(pl.multiple_of(start, 64), size)
        return ref.at[sl, :] if lead is None else ref.at[lead, sl, :]

    hu, hc = n // 2, c_ref.shape[0] // 2
    su, sc = core * hu, core * hc
    near = [
        copy(0, part(u_ref, None, su, hu), part(ug, 0, su, hu), up),
        copy(1, part(c_ref, None, sc, hc), part(cg, 0, sc, hc), up),
        copy(2, part(u_ref, None, su, hu), part(ug, 2, su, hu), down),
        copy(3, part(c_ref, None, sc, hc), part(cg, 2, sc, hc), down),
    ]
    qu, qc = hu // 2, hc // 2
    far = [
        copy(4, part(ug, 0, su, qu), part(ug, 1, su, qu), up),
        copy(5, part(cg, 0, sc, qc), part(cg, 1, sc, qc), up),
        copy(6, part(ug, 2, su + qu, qu), part(ug, 1, su + qu, qu), down),
        copy(7, part(cg, 2, sc + qc, qc), part(cg, 1, sc + qc, qc), down),
    ]
    swap = []
    for k, slot in enumerate((0, 2, 1)):
        swap.append(copy(8 + 2 * k, part(ug, slot, su, hu), part(ug, slot, su, hu), pair))
        swap.append(copy(9 + 2 * k, part(cg, slot, sc, hc), part(cg, slot, sc, hc), pair))
    for d in near:
        d.start()

    rank = c_ref.shape[0]
    k_index = lax.broadcasted_iota(jnp.int32, (rank, rank), 0)
    e_index = lax.broadcasted_iota(jnp.int32, (rank, rank), 1)
    for s in range(left_ref.shape[0]):
        keep = (k_index < ranks_ref[0, s, 0]) & (e_index < diag_rank_ref[0])
        inner = mm(right_ref[s], vd_ref[...], ((0,), (0,)))
        inner = jnp.where(keep, inner, 0.0).astype(BF)
        low_ref[s] = mm(left_ref[s], inner, ((1,), (0,))).astype(BF)

    for d in near:
        d.wait_recv()
    for d in far:
        d.start()
    for d in swap[:4]:
        d.start()

    step = 32
    line = lax.broadcasted_iota(jnp.int32, (step, n), 1)
    inside = lax.broadcasted_iota(jnp.int32, (step, n), 0)

    def fill(i, _):
        at = pl.ds(pl.multiple_of(i * step, step), step)
        block = matern(col_ref[at, 0:1], col_ref[at, 1:2], row_ref[0:1, :], row_ref[1:2, :])
        a_ref[at, :] = block + jnp.where(line == inside + i * step, nugget, 0.0)
        return 0

    lax.fori_loop(0, n // step // 2, fill, 0)
    for d in far:
        d.wait_recv()
    for d in swap[4:]:
        d.start()
    lax.fori_loop(n // step // 2, n // step, fill, 0)

    def subtract(u, c, where):
        all_ref[:, where * rank:(where + 1) * rank] = u
        wide = 256

        def chunk(i, _):
            at = pl.ds(pl.multiple_of(i * wide, wide), wide)
            low = mm(all_ref[at, where * rank:(where + 1) * rank], c, ((1,), (0,))).astype(BF)
            a_ref[at, :] = a_ref[at, :] - mm(low, u, ((1,), (1,)))
            return 0

        lax.fori_loop(0, n // wide, chunk, 0)

    subtract(u_ref[...], c_ref[...], 0)
    for k, slot in enumerate((0, 2, 1)):
        swap[2 * k].wait_recv()
        swap[2 * k + 1].wait_recv()
        subtract(ug[slot], cg[slot], slot + 1)
    for d in near + far + swap:
        d.wait_send()


def front(ranks, diag_rank, u, c, left, right, vd, col, row):
    n, rank = u.shape
    slots = left.shape[0]
    vmem = pl.BlockSpec(memory_space=pltpu.VMEM)
    return pl.pallas_call(
        front_kernel,
        out_shape=(
            jax.ShapeDtypeStruct((n, n), F32),
            jax.ShapeDtypeStruct((slots, n, rank), BF),
            jax.ShapeDtypeStruct((n, 4 * rank), BF),
        ),
        in_specs=[pl.BlockSpec(memory_space=pltpu.SMEM)] * 2 + [vmem] * 7,
        out_specs=(vmem, vmem, vmem),
        scratch_shapes=[
            pltpu.VMEM((3, n, rank), BF),
            pltpu.VMEM((3, rank, rank), BF),
            pltpu.SemaphoreType.DMA((14,)),
            pltpu.SemaphoreType.DMA((14,)),
        ],
        compiler_params=pltpu.CompilerParams(collective_id=0, has_side_effects=True, vmem_limit_bytes=60 << 20),
        name="front",
    )(ranks, diag_rank, u, c, left, right, vd, col, row)


def slot_of_tile(slot_tile, tile_count):
    flat_tiles = slot_tile.reshape(-1)
    tiles = jnp.arange(tile_count, dtype=jnp.int32)
    slots = jnp.arange(flat_tiles.shape[0], dtype=jnp.int32)
    return jnp.sum(jnp.where(flat_tiles[None, :] == tiles[:, None], slots[None, :], 0), axis=1)


def shift(x, axis, size, by):
    return lax.ppermute(x, axis, [(i, (i + by) % size) for i in range(size)])


def per_device(
    slot_tile,
    slot_ranks,
    diag_ranks,
    panel_left_factors,
    panel_v,
    diag_u,
    diag_v,
    panel_points,
    diag_points,
    rhs_diag,
    rhs_rest,
):
    row_devices = lax.axis_size("rows")
    col_devices = lax.axis_size("cols")
    slot_count = panel_left_factors.shape[1]
    tile_order = diag_u.shape[1]
    rank_max = diag_u.shape[2]
    quarter = tile_order // col_devices
    per_peer = quarter // row_devices
    tile_count = rhs_rest.shape[0]
    row_index = lax.axis_index("rows")
    col_index = lax.axis_index("cols")
    core = row_index % 2
    rank_index = jnp.arange(rank_max, dtype=jnp.int32)
    diag_mask = (rank_index < diag_ranks[0]).astype(BF)
    diagonal_right_factor = diag_v[0] * diag_mask[None, :]
    diag_core = jnp.einsum(
        "br,bq->rq", diagonal_right_factor, diagonal_right_factor, preferred_element_type=F32
    ).astype(BF)
    centre = diag_points.astype(F32)
    diag_system, low_rows, left_cat = front(
        slot_ranks, diag_ranks, diag_u[0], diag_core, panel_left_factors[0], panel_v[0], diag_v[0], centre.T, centre
    )
    low_parts = []
    for by in range(col_devices):
        target = (col_index + by) % col_devices
        part = lax.dynamic_slice_in_dim(low_rows, target * quarter, quarter, 1)
        low_parts.append(shift(part, "cols", col_devices, by) if by else part)
    half = tile_order // 2
    rhs_mine = jnp.where(core == 0, rhs_diag[:half], rhs_diag[half:])
    rhs_mine, diag_system = lax.optimization_barrier((rhs_mine, diag_system))
    rhs_got = jnp.stack([shift(rhs_mine, "cols", col_devices, by) for by in range(1, col_devices)])
    inverse = chol_inv(diag_system)
    inverse, low_parts, rhs_got = lax.optimization_barrier((inverse, low_parts, rhs_got))
    rhs_other = lax.ppermute(rhs_got, "rows", [(i, i ^ 1) for i in range(row_devices)])
    rhs_all = [rhs_diag] + [
        jnp.concatenate([jnp.where(core == 0, g, o), jnp.where(core == 0, o, g)], axis=0)
        for g, o in zip(rhs_got, rhs_other)
    ]
    rhs_cat = jnp.concatenate(rhs_all, axis=1)
    update_term = jnp.einsum(
        "snr,br->snb", jnp.concatenate(low_parts, axis=2), left_cat, preferred_element_type=F32
    )
    is_mine = jnp.arange(row_devices, dtype=jnp.int32)[:, None] == row_index
    my_tiles = jnp.sum(jnp.where(is_mine, slot_tile, 0), axis=0)
    live_mask = (my_tiles < tile_count).astype(F32)
    coords = panel_points.astype(F32)
    generated = matern(coords[:, 0, :, None], coords[:, 1, :, None], centre[0], centre[1])
    system_rows = live_mask[:, None, None] * (generated - update_term)
    system_rows = system_rows.reshape(slot_count * quarter, tile_order)
    sys_hi, sys_lo = split2_outside(system_rows)
    inv_hi, inv_lo = split2_outside(inverse)
    rhs_hi, rhs_lo = split2_outside(rhs_cat)
    panel_blocks = []
    solution_blocks = []
    step = 256
    for lo in range(0, tile_order, step):
        hi = lo + step
        a_hi, a_lo = sys_hi[:, :hi], sys_lo[:, :hi]
        b_hi, b_lo = inv_hi[lo:hi, :hi], inv_lo[lo:hi, :hi]
        dims = ((1,), (1,))
        panel_blocks.append((mm(a_hi, b_hi, dims) + (mm(a_hi, b_lo, dims) + mm(a_lo, b_hi, dims))).astype(BF))
        dims = ((1,), (0,))
        r_hi, r_lo = rhs_hi[:hi], rhs_lo[:hi]
        solution_blocks.append(mm(b_hi, r_hi, dims) + (mm(b_hi, r_lo, dims) + mm(b_lo, r_hi, dims)))
    panel_factor = jnp.concatenate(panel_blocks, axis=1)
    solution_all = jnp.concatenate(solution_blocks, axis=0)
    width = rhs_diag.shape[1]
    diag_solution = solution_all[:, :width]
    total = width * col_devices
    source = jnp.arange(total, dtype=jnp.int32)[:, None]
    place = jnp.arange(total, dtype=jnp.int32)[None, :]
    belongs = (col_index + col_devices - source // width) % col_devices == place // width
    order = (belongs & (source % width == place % width)).astype(BF)
    forward = jnp.dot(solution_all.astype(BF), order, preferred_element_type=F32).astype(BF)
    product = jnp.dot(panel_factor, forward, preferred_element_type=F32).astype(BF)
    outgoing = product.reshape(slot_count, per_peer, row_devices, forward.shape[1])
    incoming = lax.all_to_all(outgoing, "rows", split_axis=2, concat_axis=2, tiled=True)
    owner_slot = slot_of_tile(slot_tile, tile_count)
    source_row = owner_slot // slot_count
    source_place = owner_slot % slot_count
    step_index = jnp.arange(per_peer, dtype=jnp.int32)
    pick = ((source_place[:, None] * per_peer + step_index[None, :]) * row_devices + source_row[:, None]).reshape(-1)
    picked = jnp.take(incoming.reshape(-1, forward.shape[1]), pick, axis=0)
    rhs_out = rhs_rest - picked.reshape(rhs_rest.shape).astype(F32)
    return (panel_factor.reshape(slot_count, quarter, tile_order), diag_solution, rhs_out)


def solution(mesh):
    return jax.shard_map(
        per_device,
        mesh=mesh,
        in_specs=(
            P(),
            P("rows", None, "cols"),
            P("cols"),
            P("cols", "rows", None, None),
            P("cols", "rows", None, None),
            P("cols", None, None),
            P("cols", None, None),
            P("rows", None, "cols"),
            P(),
            P(None, "cols"),
            P(None, "cols", None, "rows", None),
        ),
        out_specs=(P("rows", "cols", None), P(None, "cols"), P(None, "cols", None, "rows", None)),
        check_vma=False,
    )
```

```python
import functools

import jax
import jax.numpy as jnp
from jax import lax
from jax.experimental import pallas as pl
from jax.experimental.pallas import tpu as pltpu
from jax.sharding import PartitionSpec as P

GX = 1024

length_scale = 0.3
nugget = 1.0
F32 = jnp.float32
BF = jnp.bfloat16
HI = lax.Precision.HIGHEST


def split2(x):
    hi = x.astype(BF)
    lo = (x - hi.astype(F32)).astype(BF)
    return hi, lo


def mm(a, b, dims):
    return lax.dot_general(a, b, (dims, ((), ())), preferred_element_type=F32)


def mm3(a, b, dims):
    ah, al = split2(a)
    bh, bl = split2(b)
    return mm(ah, bh, dims) + (mm(ah, bl, dims) + mm(al, bh, dims))


def factor_block(rows, lin_ref):
    n = len(rows)
    rows = list(rows)
    lane = lax.broadcasted_iota(jnp.int32, (8, 128), 1)
    sub = lax.broadcasted_iota(jnp.int32, (8, 128), 0)
    bs = lambda x, k: jnp.broadcast_to(x[k:k + 1, :], (8, 128))
    for b in range(n):
        inblock = (lane >= 8 * b) & (lane < 8 * b + 8)
        t = rows[b]
        c = [jnp.broadcast_to(t[:, 8 * b + k:8 * b + k + 1], (8, 128)) for k in range(8)]
        tm = jnp.where(inblock, (lane - 8 * b == sub).astype(F32), t)
        y = tm
        scale = jnp.ones((8, 128), F32)
        avec = jnp.ones((8, 128), F32)
        bvec = jnp.zeros((8, 128), F32)
        for k in range(0, 8, 2):
            ck, cl = c[k], c[k + 1]
            pa, pb, pc = bs(ck, k), bs(ck, k + 1), bs(cl, k + 1)
            det = pa * pc - pb * pb
            r = 1.0 / det
            ek = pc * ck - pb * cl
            fk = pa * cl - pb * ck
            wk, wl = ek * r, fk * r
            at_k, at_l = sub == k, sub == k + 1
            scale = jnp.where(at_k, pa, jnp.where(at_l, pa * det, scale))
            avec = jnp.where(at_l, pa, avec)
            bvec = jnp.where(at_l, pb, bvec)
            if k < 6:
                below = sub > k + 1
                y = y - jnp.where(below, wk * bs(y, k) + wl * bs(y, k + 1), 0.0)
            new = list(c)
            for m in range(8):
                if m in (k, k + 1):
                    continue
                g = ck * bs(ek, m) + cl * bs(fk, m)
                v = c[m] - g * r
                new[m] = jnp.where(at_k, bs(wk, m), jnp.where(at_l, bs(wl, m), v))
            new[k] = jnp.where(at_k, -pc * r, jnp.where(at_l, pb * r, wk))
            new[k + 1] = jnp.where(at_k, pb * r, jnp.where(at_l, -pa * r, wl))
            c = new
        if b < n - 1:
            s = [c[m] * bs(tm, m) for m in range(8)]
            s = ((s[0] + s[1]) + (s[2] + s[3])) + ((s[4] + s[5]) + (s[6] + s[7]))
            sk = [bs(s, k) for k in range(8)]
            for i in range(b + 1, n):
                q = [jnp.broadcast_to(rows[i][:, 8 * b + k:8 * b + k + 1], (8, 128)) * sk[k] for k in range(8)]
                q = ((q[0] + q[1]) + (q[2] + q[3])) + ((q[4] + q[5]) + (q[6] + q[7]))
                rows[i] = jnp.where(inblock, 0.0, rows[i]) + q
        yy = avec * y - bvec * pltpu.roll(y, 1, 0)
        res = yy * lax.rsqrt(scale)
        lin_ref[8 * b:8 * b + 8, :] = jnp.where(lane < 8 * b + 8, res, 0.0)


def chol_inv_kernel(a_ref, hi_ref, lo_ref, x_ref, lin_ref, *, n, passes):
    nb = n // 128
    x_ref[...] = a_ref[...]
    dot = mm3 if passes == 3 else functools.partial(lambda a, b, dims: lax.dot_general(a, b, (dims, ((), ())), preferred_element_type=F32, precision=HI))

    def body(p, _):
        off = pl.multiple_of(p * 128, 128)
        rows = [x_ref[pl.ds(pl.multiple_of(off + 8 * b, 8), 8), pl.ds(off, 128)] for b in range(16)]
        factor_block(rows, lin_ref)
        lin = lin_ref[...]
        for q in range(nb):
            @pl.when(p == q)
            def _():
                lo, hi = 128 * q, 128 * (q + 1)
                left = None
                if q < nb - 1:
                    left = dot(x_ref[hi:, lo:hi], lin, ((1,), (1,)))
                    right = dot(lin, x_ref[lo:hi, hi:], ((1,), (0,)))
                    x_ref[lo:hi, hi:] = jnp.zeros((128, n - hi), F32)
                if q > 0:
                    x_ref[lo:hi, :lo] = dot(lin, x_ref[lo:hi, :lo], ((1,), (0,)))
                x_ref[lo:hi, lo:hi] = lin
                if q < nb - 1:
                    x_ref[hi:, hi:] = x_ref[hi:, hi:] - dot(left, right, ((1,), (0,)))
                    if q > 0:
                        x_ref[hi:, :lo] = x_ref[hi:, :lo] - dot(left, x_ref[lo:hi, :lo], ((1,), (0,)))
                    x_ref[hi:, lo:hi] = -dot(left, lin, ((1,), (0,)))
        return 0

    lax.fori_loop(0, nb, body, 0)

    def store(i, _):
        at = pl.ds(pl.multiple_of(i * 32, 32), 32)
        hi_ref[at, :], lo_ref[at, :] = split2(x_ref[at, :])
        return 0

    lax.fori_loop(0, n // 32, store, 0)


def chol_inv(a, passes=3):
    n = a.shape[0]
    return pl.pallas_call(
        functools.partial(chol_inv_kernel, n=n, passes=passes),
        out_shape=(jax.ShapeDtypeStruct((n, n), BF), jax.ShapeDtypeStruct((n, n), BF)),
        in_specs=[pl.BlockSpec(memory_space=pltpu.VMEM)],
        out_specs=(pl.BlockSpec(memory_space=pltpu.VMEM), pl.BlockSpec(memory_space=pltpu.VMEM)),
        scratch_shapes=[pltpu.VMEM((n, n), F32), pltpu.VMEM((128, 128), F32)],
        compiler_params=pltpu.CompilerParams(vmem_limit_bytes=60 << 20),
        name="chol_inv",
        cost_estimate=pl.CostEstimate(flops=24 * n * n * n, bytes_accessed=8 * n * n, transcendentals=0),
    )(a)


def split2_outside(x):
    hi = lax.reduce_precision(x, 8, 7)
    return hi.astype(BF), lax.reduce_precision(x - hi, 8, 7).astype(BF)


def matern(first_x, first_y, second_x, second_y):
    delta_x = first_x - second_x
    delta_y = first_y - second_y
    scaled = jnp.sqrt(delta_x * delta_x + delta_y * delta_y) * (3.0**0.5 / (GX * length_scale))
    return (1.0 + scaled) * jnp.exp(-scaled)


MESH = pl.DeviceIdType.MESH


def front_kernel(
    ranks_ref, diag_rank_ref, u_ref, c_ref, left_ref, right_ref, vd_ref, col_ref, row_ref,
    a_ref, low_ref, all_ref,
    ug, cg, send, recv,
):
    n = u_ref.shape[0]
    rows, cols = lax.axis_index("rows"), lax.axis_index("cols")
    count = lax.axis_size("cols")
    core = lax.rem(rows, 2)
    up = {"cols": lax.rem(cols + 1, count)}
    down = {"cols": lax.rem(cols + count - 1, count)}
    pair = {"rows": rows + 1 - 2 * core}

    barrier = pltpu.get_barrier_semaphore()
    for peer in (up, down, pair):
        pl.semaphore_signal(barrier, inc=1, device_id=peer, device_id_type=MESH)
    pl.semaphore_wait(barrier, 3)

    def copy(k, src, dst, peer):
        return pltpu.make_async_remote_copy(
            src_ref=src, dst_ref=dst, send_sem=send.at[k], recv_sem=recv.at[k], device_id=peer, device_id_type=MESH
        )

    def part(ref, lead, start, size):
        sl = pl.ds(pl.multiple_of(start, 64), size)
        return ref.at[sl, :] if lead is None else ref.at[lead, sl, :]

    hu, hc = n // 2, c_ref.shape[0] // 2
    su, sc = core * hu, core * hc
    near = [
        copy(0, part(u_ref, None, su, hu), part(ug, 0, su, hu), up),
        copy(1, part(c_ref, None, sc, hc), part(cg, 0, sc, hc), up),
        copy(2, part(u_ref, None, su, hu), part(ug, 2, su, hu), down),
        copy(3, part(c_ref, None, sc, hc), part(cg, 2, sc, hc), down),
    ]
    qu, qc = hu // 2, hc // 2
    far = [
        copy(4, part(ug, 0, su, qu), part(ug, 1, su, qu), up),
        copy(5, part(cg, 0, sc, qc), part(cg, 1, sc, qc), up),
        copy(6, part(ug, 2, su + qu, qu), part(ug, 1, su + qu, qu), down),
        copy(7, part(cg, 2, sc + qc, qc), part(cg, 1, sc + qc, qc), down),
    ]
    swap = []
    for k, slot in enumerate((0, 2, 1)):
        swap.append(copy(8 + 2 * k, part(ug, slot, su, hu), part(ug, slot, su, hu), pair))
        swap.append(copy(9 + 2 * k, part(cg, slot, sc, hc), part(cg, slot, sc, hc), pair))
    for d in near:
        d.start()

    rank = c_ref.shape[0]
    k_index = lax.broadcasted_iota(jnp.int32, (rank, rank), 0)
    e_index = lax.broadcasted_iota(jnp.int32, (rank, rank), 1)
    for s in range(left_ref.shape[0]):
        keep = (k_index < ranks_ref[0, s, 0]) & (e_index < diag_rank_ref[0])
        inner = mm(right_ref[s], vd_ref[...], ((0,), (0,)))
        inner = jnp.where(keep, inner, 0.0).astype(BF)
        low_ref[s] = mm(left_ref[s], inner, ((1,), (0,))).astype(BF)

    for d in near:
        d.wait_recv()
    for d in far:
        d.start()
    for d in swap[:4]:
        d.start()

    step = 32
    line = lax.broadcasted_iota(jnp.int32, (step, n), 1)
    inside = lax.broadcasted_iota(jnp.int32, (step, n), 0)

    def fill(i, _):
        at = pl.ds(pl.multiple_of(i * step, step), step)
        block = matern(col_ref[at, 0:1], col_ref[at, 1:2], row_ref[0:1, :], row_ref[1:2, :])
        a_ref[at, :] = block + jnp.where(line == inside + i * step, nugget, 0.0)
        return 0

    lax.fori_loop(0, n // step // 2, fill, 0)
    for d in far:
        d.wait_recv()
    for d in swap[4:]:
        d.start()
    lax.fori_loop(n // step // 2, n // step, fill, 0)

    def subtract(u, c, where):
        all_ref[:, where * rank:(where + 1) * rank] = u
        wide = 256

        def chunk(i, _):
            at = pl.ds(pl.multiple_of(i * wide, wide), wide)
            low = mm(all_ref[at, where * rank:(where + 1) * rank], c, ((1,), (0,))).astype(BF)
            a_ref[at, :] = a_ref[at, :] - mm(low, u, ((1,), (1,)))
            return 0

        lax.fori_loop(0, n // wide, chunk, 0)

    subtract(u_ref[...], c_ref[...], 0)
    for k, slot in enumerate((0, 2, 1)):
        swap[2 * k].wait_recv()
        swap[2 * k + 1].wait_recv()
        subtract(ug[slot], cg[slot], slot + 1)
    for d in near + far + swap:
        d.wait_send()


def front(ranks, diag_rank, u, c, left, right, vd, col, row):
    n, rank = u.shape
    slots = left.shape[0]
    vmem = pl.BlockSpec(memory_space=pltpu.VMEM)
    return pl.pallas_call(
        front_kernel,
        out_shape=(
            jax.ShapeDtypeStruct((n, n), F32),
            jax.ShapeDtypeStruct((slots, n, rank), BF),
            jax.ShapeDtypeStruct((n, 4 * rank), BF),
        ),
        in_specs=[pl.BlockSpec(memory_space=pltpu.SMEM)] * 2 + [vmem] * 7,
        out_specs=(vmem, vmem, vmem),
        scratch_shapes=[
            pltpu.VMEM((3, n, rank), BF),
            pltpu.VMEM((3, rank, rank), BF),
            pltpu.SemaphoreType.DMA((14,)),
            pltpu.SemaphoreType.DMA((14,)),
        ],
        compiler_params=pltpu.CompilerParams(collective_id=0, has_side_effects=True, vmem_limit_bytes=60 << 20),
        name="front",
    )(ranks, diag_rank, u, c, left, right, vd, col, row)


def slot_of_tile(slot_tile, tile_count):
    flat_tiles = slot_tile.reshape(-1)
    tiles = jnp.arange(tile_count, dtype=jnp.int32)
    slots = jnp.arange(flat_tiles.shape[0], dtype=jnp.int32)
    return jnp.sum(jnp.where(flat_tiles[None, :] == tiles[:, None], slots[None, :], 0), axis=1)


def shift(x, axis, size, by):
    return lax.ppermute(x, axis, [(i, (i + by) % size) for i in range(size)])


def per_device(
    slot_tile,
    slot_ranks,
    diag_ranks,
    panel_left_factors,
    panel_v,
    diag_u,
    diag_v,
    panel_points,
    diag_points,
    rhs_diag,
    rhs_rest,
):
    row_devices = lax.axis_size("rows")
    col_devices = lax.axis_size("cols")
    slot_count = panel_left_factors.shape[1]
    tile_order = diag_u.shape[1]
    rank_max = diag_u.shape[2]
    quarter = tile_order // col_devices
    per_peer = quarter // row_devices
    tile_count = rhs_rest.shape[0]
    row_index = lax.axis_index("rows")
    col_index = lax.axis_index("cols")
    core = row_index % 2
    rank_index = jnp.arange(rank_max, dtype=jnp.int32)
    diag_mask = (rank_index < diag_ranks[0]).astype(BF)
    diagonal_right_factor = diag_v[0] * diag_mask[None, :]
    diag_core = jnp.einsum(
        "br,bq->rq", diagonal_right_factor, diagonal_right_factor, preferred_element_type=F32
    ).astype(BF)
    centre = diag_points.astype(F32)
    diag_system, low_rows, left_cat = front(
        slot_ranks, diag_ranks, diag_u[0], diag_core, panel_left_factors[0], panel_v[0], diag_v[0], centre.T, centre
    )
    low_parts = []
    for by in range(col_devices):
        target = (col_index + by) % col_devices
        part = lax.dynamic_slice_in_dim(low_rows, target * quarter, quarter, 1)
        low_parts.append(shift(part, "cols", col_devices, by) if by else part)
    half = tile_order // 2
    rhs_mine = jnp.where(core == 0, rhs_diag[:half], rhs_diag[half:])
    rhs_mine, diag_system = lax.optimization_barrier((rhs_mine, diag_system))
    rhs_got = jnp.stack([shift(rhs_mine, "cols", col_devices, by) for by in range(1, col_devices)])
    inv_hi, inv_lo = chol_inv(diag_system)
    inv_hi, inv_lo, low_parts, rhs_got = lax.optimization_barrier((inv_hi, inv_lo, low_parts, rhs_got))
    rhs_other = lax.ppermute(rhs_got, "rows", [(i, i ^ 1) for i in range(row_devices)])
    rhs_all = [rhs_diag] + [
        jnp.concatenate([jnp.where(core == 0, g, o), jnp.where(core == 0, o, g)], axis=0)
        for g, o in zip(rhs_got, rhs_other)
    ]
    rhs_cat = jnp.concatenate(rhs_all, axis=1)
    update_term = jnp.einsum(
        "snr,br->snb", jnp.concatenate(low_parts, axis=2), left_cat, preferred_element_type=F32
    )
    is_mine = jnp.arange(row_devices, dtype=jnp.int32)[:, None] == row_index
    my_tiles = jnp.sum(jnp.where(is_mine, slot_tile, 0), axis=0)
    live_mask = (my_tiles < tile_count).astype(F32)
    coords = panel_points.astype(F32)
    generated = matern(coords[:, 0, :, None], coords[:, 1, :, None], centre[0], centre[1])
    system_rows = live_mask[:, None, None] * (generated - update_term)
    system_rows = system_rows.reshape(slot_count * quarter, tile_order)
    sys_hi, sys_lo = split2_outside(system_rows)
    rhs_hi, rhs_lo = split2_outside(rhs_cat)
    panel_blocks = []
    solution_blocks = []
    step = 256
    for lo in range(0, tile_order, step):
        hi = lo + step
        a_hi, a_lo = sys_hi[:, :hi], sys_lo[:, :hi]
        b_hi, b_lo = inv_hi[lo:hi, :hi], inv_lo[lo:hi, :hi]
        dims = ((1,), (1,))
        panel_blocks.append((mm(a_hi, b_hi, dims) + (mm(a_hi, b_lo, dims) + mm(a_lo, b_hi, dims))).astype(BF))
        dims = ((1,), (0,))
        r_hi, r_lo = rhs_hi[:hi], rhs_lo[:hi]
        solution_blocks.append(mm(b_hi, r_hi, dims) + (mm(b_hi, r_lo, dims) + mm(b_lo, r_hi, dims)))
    panel_factor = jnp.concatenate(panel_blocks, axis=1)
    solution_all = jnp.concatenate(solution_blocks, axis=0)
    width = rhs_diag.shape[1]
    diag_solution = solution_all[:, :width]
    rounded = solution_all.astype(BF)
    blocks = [rounded[:, k * width:(k + 1) * width] for k in range(col_devices)]
    ordered = []
    for place in range(col_devices):
        which = (col_index + col_devices - place) % col_devices
        chosen = blocks[-1]
        for k in range(col_devices - 1):
            chosen = jnp.where(which == k, blocks[k], chosen)
        ordered.append(chosen)
    forward = jnp.concatenate(ordered, axis=1)
    product = jnp.dot(panel_factor, forward, preferred_element_type=F32).astype(BF)
    outgoing = product.reshape(slot_count, per_peer, row_devices, forward.shape[1])
    incoming = lax.all_to_all(outgoing, "rows", split_axis=2, concat_axis=2, tiled=True)
    owner_slot = slot_of_tile(slot_tile, tile_count)
    source_row = owner_slot // slot_count
    source_place = owner_slot % slot_count
    step_index = jnp.arange(per_peer, dtype=jnp.int32)
    pick = ((source_place[:, None] * per_peer + step_index[None, :]) * row_devices + source_row[:, None]).reshape(-1)
    picked = jnp.take(incoming.reshape(-1, forward.shape[1]), pick, axis=0)
    rhs_out = rhs_rest - picked.reshape(rhs_rest.shape).astype(F32)
    return (panel_factor.reshape(slot_count, quarter, tile_order), diag_solution, rhs_out)


def solution(mesh):
    return jax.shard_map(
        per_device,
        mesh=mesh,
        in_specs=(
            P(),
            P("rows", None, "cols"),
            P("cols"),
            P("cols", "rows", None, None),
            P("cols", "rows", None, None),
            P("cols", None, None),
            P("cols", None, None),
            P("rows", None, "cols"),
            P(),
            P(None, "cols"),
            P(None, "cols", None, "rows", None),
        ),
        out_specs=(P("rows", "cols", None), P(None, "cols"), P(None, "cols", None, "rows", None)),
        check_vma=False,
    )
```
